32 devices in a mesh: parts: 2 (over y), freq: 8 (over z, x), seg: 2 (over core).
Axes of the slice: x: 2, y: 2, z: 4, core: 2. Of those that a mesh axis runs over, the one named last changes fastest.
Arguments:
- samples: float32 [8, 2, 1024, 1024], P(('parts', 'seg'), None, 'freq'), parts along dimension 0, may hold values from -6 to 6
- kernels: bfloat16 [2, 8, 128], replicated, may hold values from -0.375 to 0.375
- offsets: int32 [8, 8], P(('parts', 'seg')), parts along dimension 0, may hold values from -4096 to 4096, as said below
- weight_index: int32 [8], P(('parts', 'seg')), parts along dimension 0, may hold values from 0 to 15
- level_weights: float32 [16], replicated, may hold values from 0.1 to 1
Outputs:
- planes: float32 [16, 1048576], P(('parts', 'seg'), 'freq'), parts along dimension 0
The draws below stay inside these ranges and needn't reach their ends.
There are 2 independent parts, one for each index of `parts`. The reference program is written for one: setup_inputs(seed, part) draws one part's arguments, and reference() takes and returns one part's arrays. A program takes and returns all parts, laid end to end along the dimension named above; an argument that names none is the same for every part. Nothing has to cross between parts.
Inputs may be any that keep to these rules, and one draw needn't show every extreme that they name: `offsets`: each offset lies within 4096 blocks of zero; both ends are taken in every draw. Among the 16 offsets of one index of seg, at most 4 have the same quotient by 1024 (rounded down), and in every draw some quotient has exactly 4.
All inputs are finite; a program needn't handle non-finite values.
Results may differ from the reference program's by a relative error of at most 0.01.
Values may be sent and summed in bfloat16 or wider, within the bound.
A program may use at most 128 MiB of HBM per device.

```python
import math
import jax
import jax.numpy as jnp
from jax import lax

N1 = 1024
N2 = 1024
BLOCK = 128
KERNELS = 8
REACH = 4
LEVELS = 16
SEG_DEV = 2
SEGMENTS = 4
BLOCKS_DEV = 1024
ROUTE_CAP = 4


def offsets_group(group_key):
    planes_one = SEG_DEV * KERNELS
    spread = 2 * REACH + 1
    slots = spread * ROUTE_CAP
    centre = jax.random.randint(jax.random.fold_in(group_key, 1), (), -REACH + 1, REACH)
    slot_dist = jnp.repeat(jnp.arange(spread, dtype=jnp.int32) - REACH, ROUTE_CAP)
    slot_rank = jnp.tile(jnp.arange(ROUTE_CAP, dtype=jnp.int32), spread)
    noise = jax.random.permutation(jax.random.fold_in(group_key, 2), slots).astype(jnp.int32)
    extreme = ((slot_dist == REACH) | (slot_dist == -REACH)) & (slot_rank == 0)
    priority = jnp.where(slot_dist == centre, 0, jnp.where(extreme, 1, 2)).astype(jnp.int32)
    order = jnp.argsort(priority * slots + noise, stable=True)
    chosen = slot_dist[order[:planes_one]]
    placing = jax.random.permutation(jax.random.fold_in(group_key, 3), planes_one)
    quotient = jnp.zeros((planes_one,), jnp.int32).at[placing].set(chosen)
    remainder = jax.random.randint(jax.random.fold_in(group_key, 4), (planes_one,), 0, BLOCKS_DEV)
    remainder = jnp.where(jnp.abs(quotient) == REACH, 0, remainder)
    return (quotient * BLOCKS_DEV + remainder).astype(jnp.int32)


def draw_offsets(key, part):
    groups = SEGMENTS // SEG_DEV
    keys = jax.vmap(lambda number: jax.random.fold_in(key, number))(jnp.arange(groups, dtype=jnp.int32) + 11)
    values = jax.vmap(offsets_group)(keys)
    return values.reshape(SEGMENTS, KERNELS).astype(jnp.int32)


def plant(drawn, stream_key, least, top_value):
    index_at = [jax.random.randint(jax.random.fold_in(stream_key, axis), (), 0, length) for axis, length in enumerate(drawn.shape)]
    main_axis = drawn.shape.index(max(drawn.shape))
    neighbour = index_at[:main_axis] + [(index_at[main_axis] + 1) % drawn.shape[main_axis]] + index_at[main_axis + 1:]
    return drawn.at[tuple(index_at)].set(least).at[tuple(neighbour)].set(top_value)


def block_scale(own_key, extent, pieces, low, largest):
    def one(axis_at, shards_of):
        draws = jax.random.uniform(jax.random.fold_in(jax.random.fold_in(own_key, 6), axis_at), (shards_of,), jnp.float32, low / len(pieces), largest / len(pieces))
        return jnp.repeat(jnp.exp(draws), extent[axis_at] // shards_of).reshape((-1,) + (1,) * (len(extent) - axis_at - 1))

    factor_of = one(*pieces[0])
    for cut in pieces[1:]:
        factor_of = factor_of * one(*cut)
    return factor_of


def bell_draw(own_key, extent, width, bound, shards=(), kind=jnp.bfloat16):
    drawn = jax.random.normal(own_key, extent, jnp.float32) * width
    if len(shards) > 0:
        drawn = block_scale(own_key, extent, shards, -0.22, 0.18) * drawn
    return jnp.clip(drawn, min=-bound, max=bound).astype(kind)


def setup_inputs(seed: int = 0, part: int = 0) -> dict:
    streams_of = jax.random.split(jax.random.key(seed), 6)
    own_keys = jax.random.split(jax.random.fold_in(streams_of[5], part), 6)
    samples = bell_draw(own_keys[0], (SEGMENTS, 2, N1, N2), 1.0, 6.0, ((0, 2), (2, 8)), jnp.float32)
    kernels = bell_draw(streams_of[1], (2, KERNELS, BLOCK), (2 * BLOCK) ** -0.5, 0.375)
    offsets = draw_offsets(jax.random.fold_in(jax.random.fold_in(streams_of[5], part), 71), part)
    weight_index = plant(jax.random.randint(own_keys[3], (SEGMENTS,), 0, LEVELS), jax.random.fold_in(own_keys[3], 1), 0, LEVELS - 1).astype(jnp.int32)
    level_weights = jnp.clip(jnp.exp(jax.random.uniform(streams_of[4], (LEVELS,), jnp.float32, math.log(0.1), math.log(1.0))), 0.1, 1.0)
    return dict(samples=samples, kernels=kernels, offsets=offsets, weight_index=weight_index, level_weights=level_weights)


def reference(samples, kernels, offsets, weight_index, level_weights):
    length = N1 * N2
    half = BLOCK // 2
    places = (half - jnp.arange(BLOCK, dtype=jnp.int32)) % length
    kernel_real = kernels[0].astype(jnp.float32)
    kernel_imag = kernels[1].astype(jnp.float32)
    kernel_full = kernel_real + 1j * kernel_imag
    padded = jnp.zeros((KERNELS, length), kernel_full.dtype).at[:, places].set(kernel_full)
    kernel_freq = jnp.fft.fft(padded, axis=-1)
    weights = level_weights[weight_index]

    def roll_blocks(blocks, shift):
        return jnp.roll(blocks, -shift, axis=0)

    def one_segment(total, inputs):
        segment, shifts, weight = inputs
        series = jnp.transpose(segment[0]).reshape(-1) + 1j * jnp.transpose(segment[1]).reshape(-1)
        spectrum = jnp.fft.fft(series) / math.sqrt(length)
        real_part = lax.optimization_barrier(jnp.real(spectrum).astype(jnp.bfloat16)).astype(jnp.float32)
        imag_part = lax.optimization_barrier(jnp.imag(spectrum).astype(jnp.bfloat16)).astype(jnp.float32)
        rounded = real_part + 1j * imag_part
        filtered = jnp.fft.ifft(jnp.fft.fft(rounded)[None, :] * kernel_freq, axis=-1)
        power = jnp.real(filtered) ** 2 + jnp.imag(filtered) ** 2
        power = lax.optimization_barrier(power.astype(jnp.bfloat16)).astype(jnp.float32)
        blocks = power.reshape(KERNELS, length // BLOCK, BLOCK)
        moved = jax.vmap(roll_blocks)(blocks, shifts)
        return (total + weight * moved, None)
    start = jnp.zeros((KERNELS, length // BLOCK, BLOCK), jnp.float32)
    total, unused = lax.scan(one_segment, start, (samples, offsets, weights))
    return (total / SEGMENTS).reshape(KERNELS, length)
```

```python
import math

import functools

import jax
import jax.numpy as jnp
import numpy as np
from jax import lax
from jax.experimental import pallas as pl
from jax.experimental.pallas import tpu as pltpu
from jax.sharding import PartitionSpec as P

BLOCK = 128
KERNELS = 8
REACH = 4
ROUTE_CAP = 4


def extended(cells, sides, width):
    for axis, dim in sides:
        count = lax.axis_size(axis)
        head = lax.slice_in_dim(cells, 0, width, axis=dim)
        tail = lax.slice_in_dim(cells, cells.shape[dim] - width, cells.shape[dim], axis=dim)
        cells = jnp.concatenate(
            [
                lax.ppermute(tail, axis, [(i, (i + 1) % count) for i in range(count)]),
                cells,
                lax.ppermute(head, axis, [((i + 1) % count, i) for i in range(count)]),
            ],
            axis=dim,
        )
    return cells


def passed_along(block, axis, distance):
    devices = range(lax.axis_size(axis))
    route = [((i - distance) % len(devices), i) for i in devices]
    return lax.ppermute(block, axis, route)


def dft_table(size):
    rows = lax.broadcasted_iota(jnp.int32, (size, size), 0)
    cols = lax.broadcasted_iota(jnp.int32, (size, size), 1)
    angle = (rows * cols % size).astype(jnp.float32) * (2.0 * math.pi / size)
    return (jnp.cos(angle), jnp.sin(angle))


def toeplitz(kernels):
    width = kernels.shape[-1]
    tail = jnp.zeros(kernels.shape[:-1] + (width + 1,), kernels.dtype)
    padded = jnp.concatenate([kernels, tail], -1)
    tiled = jnp.tile(padded, (1, 1, width))[..., : 2 * width * width]
    return tiled.reshape(kernels.shape[:-1] + (width, 2 * width))


def take_blocks(joined, start):
    return lax.dynamic_slice_in_dim(joined, start, joined.shape[0] // 2, 0)


def slide(joined, starts):
    return jax.vmap(jax.vmap(take_blocks))(joined, starts)


def general(samples, kernels, offsets, weight_index, level_weights):
    segs, comps, rows_one, cols_two = samples.shape
    ranks = lax.axis_size("freq")
    here = lax.axis_index("freq")
    size_one = rows_one * ranks
    length = size_one * cols_two
    highest = lax.Precision.HIGHEST
    cos_two, sin_two = dft_table(cols_two)
    stacked = samples.reshape(segs * comps * rows_one, cols_two)
    with_cos = jnp.dot(stacked, cos_two, precision=highest).reshape(samples.shape)
    with_sin = jnp.dot(stacked, sin_two, precision=highest).reshape(samples.shape)
    first_real = with_cos[:, 0] + with_sin[:, 1]
    first_imag = with_cos[:, 1] - with_sin[:, 0]
    row_global = here * rows_one + lax.broadcasted_iota(jnp.int32, (rows_one, cols_two), 0)
    col_global = lax.broadcasted_iota(jnp.int32, (rows_one, cols_two), 1)
    twist = (row_global * col_global % length).astype(jnp.float32) * (2.0 * math.pi / length)
    twist_cos = jnp.cos(twist)
    twist_sin = jnp.sin(twist)
    turned = jnp.stack(
        [
            first_real * twist_cos + first_imag * twist_sin,
            first_imag * twist_cos - first_real * twist_sin,
        ],
        1,
    )
    columns = lax.all_to_all(
        turned.astype(jnp.bfloat16), "freq", split_axis=3, concat_axis=3, tiled=True
    ).astype(turned.dtype)
    width_two = cols_two // ranks
    ordered = columns.reshape(segs, comps, rows_one, ranks, width_two)
    cos_one, sin_one = dft_table(size_one)
    cos_one = cos_one.reshape(ranks, rows_one, size_one)
    sin_one = sin_one.reshape(ranks, rows_one, size_one)
    second_cos = jnp.einsum("scirl,rik->sclk", ordered, cos_one, precision=highest)
    second_sin = jnp.einsum("scirl,rik->sclk", ordered, sin_one, precision=highest)
    second = jnp.stack(
        [second_cos[:, 0] + second_sin[:, 1], second_cos[:, 1] - second_sin[:, 0]], 1
    )
    arrived = lax.all_to_all(
        second.astype(jnp.bfloat16), "freq", split_axis=3, concat_axis=3, tiled=True
    ).astype(second.dtype)
    width_one = size_one // ranks
    spectrum = arrived.reshape(segs, comps, width_two, ranks, width_one)
    spectrum = jnp.transpose(spectrum, (0, 1, 4, 3, 2)).reshape(segs, comps, width_one * cols_two)
    spectrum = (spectrum * (1.0 / math.sqrt(length))).astype(jnp.bfloat16)
    half = BLOCK // 2
    edged = extended(spectrum, (("freq", 2),), half)
    bins_here = spectrum.shape[2]
    count = bins_here // BLOCK
    lower = edged[..., :bins_here].reshape(segs, comps, count, BLOCK)
    upper = edged[..., BLOCK:].reshape(segs, comps, count, BLOCK)
    window = jnp.concatenate([lower, upper], -1)
    bands = toeplitz(kernels)
    real_band = bands[0]
    imag_band = bands[1]
    table = jnp.stack(
        [jnp.stack([real_band, imag_band], 0), jnp.stack([-imag_band, real_band], 0)], 0
    )
    filtered = jnp.einsum("scbm,cokim->skboi", window, table, preferred_element_type=jnp.float32)
    power = (filtered[:, :, :, 0] ** 2 + filtered[:, :, :, 1] ** 2).astype(jnp.bfloat16)
    quotient = jnp.floor_divide(offsets, count)
    remainder = offsets - quotient * count
    following = passed_along(power, "freq", -1)
    inner = slide(jnp.concatenate([power, following], 2), remainder)
    plane_count = segs * KERNELS
    flat = inner.reshape(plane_count, count * BLOCK)
    plane_quot = quotient.reshape(plane_count)
    distances = lax.broadcasted_iota(jnp.int32, (2 * REACH + 1, plane_count), 0) - REACH
    member = (plane_quot[None, :] == distances).astype(jnp.int32)
    place = jnp.cumsum(member, 1) - 1
    slot_ids = lax.broadcasted_iota(jnp.int32, (2 * REACH + 1, ROUTE_CAP, plane_count), 1)
    select = ((member[:, None, :] == 1) & (place[:, None, :] == slot_ids)).astype(jnp.bfloat16)
    packed = jnp.einsum("dcp,pl->dcl", select, flat, preferred_element_type=jnp.float32).astype(
        jnp.bfloat16
    )
    received = []
    for step_index in range(2 * REACH + 1):
        received.append(passed_along(packed[step_index], "freq", -(step_index - REACH)))
    gathered = jnp.stack(received, 0)
    placed = jnp.einsum("dcp,dcl->pl", select, gathered, preferred_element_type=jnp.float32)
    shifted = placed.astype(jnp.bfloat16).reshape(segs, KERNELS, count, BLOCK)
    levels = lax.broadcasted_iota(jnp.int32, (segs, level_weights.shape[0]), 1)
    weights = jnp.sum(jnp.where(weight_index[:, None] == levels, level_weights[None, :], 0.0), 1)
    scale = 1.0 / (segs * lax.axis_size("seg"))
    partial_sum = jnp.sum((weights * scale)[:, None, None, None] * shifted.astype(jnp.float32), 0)
    owned = lax.psum_scatter(
        partial_sum.astype(jnp.bfloat16), "seg", scatter_dimension=0, tiled=True
    ).astype(jnp.float32)
    return owned.reshape(owned.shape[0], count * BLOCK)


VMEM = pl.BlockSpec(memory_space=pltpu.VMEM)
SMEM = pl.BlockSpec(memory_space=pltpu.SMEM)
PAD = 16
BF16 = jnp.bfloat16
F32 = jnp.float32


def unit(turns, scale=1.0):
    angle = 2.0 * np.pi * turns
    return (np.cos(angle) * scale).astype(np.float32), (np.sin(angle) * scale).astype(np.float32)


def wave_bases(size, first):
    step = math.isqrt(size)
    while size % step:
        step -= 1
    cols = np.arange(size) + first
    low = np.arange(step)[:, None] * cols[None, :] % size / size
    high = np.arange(size // step)[:, None] * step * cols[None, :] % size / size
    return unit(low) + unit(high)


def fill_waves(low_cos, low_sin, high_cos, high_sin, cos_ref, sin_ref):
    step = low_cos.shape[0]

    @pl.loop(0, high_cos.shape[0])
    def _(i):
        hc = high_cos[pl.ds(i, 1), :]
        hs = high_sin[pl.ds(i, 1), :]
        lc = low_cos[...]
        ls = low_sin[...]
        rows = pl.ds(pl.multiple_of(i * step, step), step)
        cos_ref[rows, :] = (hc * lc - hs * ls).astype(BF16)
        sin_ref[rows, :] = (hs * lc + hc * ls).astype(BF16)


def first_kernel(x_ref, lc, ls, hc, hs, tc, ts, dc, ds_, out_ref, cos_ref, sin_ref, xb_ref, far_ref):
    segs, comps, rows, cols = x_ref.shape
    here = lax.axis_index("freq")
    fill_waves(lc, ls, hc, hs, cos_ref, sin_ref)
    far_ref[0:1, :] = dc[pl.ds(here, 1), :]
    far_ref[8:9, :] = ds_[pl.ds(here, 1), :]
    for s in range(segs):
        for c in range(comps):
            at = (s * comps + c) * rows
            xb_ref[at : at + rows, :] = x_ref[s, c].astype(BF16)

    @pl.loop(0, out_ref.shape[0])
    def _(j):
        lanes = pl.ds(pl.multiple_of(j * BLOCK, BLOCK), BLOCK)
        rhs = jnp.concatenate([cos_ref[:, lanes], sin_ref[:, lanes]], 1)
        got = jnp.dot(xb_ref[...], rhs, preferred_element_type=F32)
        a = far_ref[0:1, lanes]
        b = far_ref[8:9, lanes]
        wc = a * tc[:, lanes] - b * ts[:, lanes]
        ws = b * tc[:, lanes] + a * ts[:, lanes]
        for s in range(segs):
            top = got[2 * s * rows : (2 * s + 1) * rows]
            bottom = got[(2 * s + 1) * rows : (2 * s + 2) * rows]
            re = top[:, :BLOCK] + bottom[:, BLOCK:]
            im = bottom[:, :BLOCK] - top[:, BLOCK:]
            out_ref[j, s, 0] = (re * wc + im * ws).astype(BF16)
            out_ref[j, s, 1] = (im * wc - re * ws).astype(BF16)


def second_kernel(x_ref, lc, ls, hc, hs, out_ref, cos_ref, sin_ref, rhs_ref):
    ranks, segs, comps, rows, width = x_ref.shape
    fill_waves(lc, ls, hc, hs, cos_ref, sin_ref)
    for d in range(ranks):
        for s in range(segs):
            for c in range(comps):
                at = (s * comps + c) * width
                rhs_ref[d * rows : (d + 1) * rows, at : at + width] = x_ref[d, s, c]

    @pl.loop(0, ranks)
    def _(i):
        here = pl.ds(pl.multiple_of(i * rows, rows), rows)
        yc = jnp.dot(cos_ref[here, :], rhs_ref[...], preferred_element_type=F32)
        ys = jnp.dot(sin_ref[here, :], rhs_ref[...], preferred_element_type=F32)
        for s in range(segs):
            re, im = 2 * s * width, (2 * s + 1) * width
            out_ref[s, 0, here] = (yc[:, re : re + width] + ys[:, im : im + width]).astype(BF16)
            out_ref[s, 1, here] = (yc[:, im : im + width] - ys[:, re : re + width]).astype(BF16)


def fill_bands(u_ref, band_ref):
    wide = 2 * BLOCK

    @pl.loop(0, u_ref.shape[1])
    def _(t):
        both = []
        for c in range(2):
            row = jnp.broadcast_to(u_ref[c, pl.ds(t, 1), :], (wide, wide))
            both.append(pltpu.roll(row, 0, 1, stride=1, stride_axis=0)[:, :BLOCK])
        re, im = both
        band_ref[t, :wide, :BLOCK] = re.astype(BF16)
        band_ref[t, :wide, BLOCK:] = im.astype(BF16)
        band_ref[t, wide:, :BLOCK] = (-im).astype(BF16)
        band_ref[t, wide:, BLOCK:] = re.astype(BF16)


def filter_one(w_ref, band_ref, p_ref, off_ref, s, t, rows, ranks):
    total = w_ref.shape[3] - rows - PAD
    here = lax.axis_index("freq")
    blocks = total * ranks
    base = lax.rem(here * rows * ranks + off_ref[s, t] + blocks, blocks)
    gk = base // ranks
    gj = base - gk * ranks
    tall = rows + PAD
    parts = []
    shifts = []
    for jj in range(ranks):
        jv = gj + jj
        carry = (jv >= ranks).astype(jnp.int32)
        j = jv - carry * ranks
        row = lax.rem(gk + carry, total)
        low = row // PAD * PAD
        shifts.append(row - low)
        take = pl.ds(pl.multiple_of(low, PAD), tall)
        parts.append(
            jnp.concatenate(
                [w_ref[s, 0, j, take, :], w_ref[s, 0, j + 1, take, :], w_ref[s, 1, j, take, :], w_ref[s, 1, j + 1, take, :]],
                1,
            )
        )
    got = jnp.dot(jnp.concatenate(parts, 0), band_ref[t], preferred_element_type=F32)
    re = got[:, :BLOCK]
    im = got[:, BLOCK:]
    p_ref[...] = re * re + im * im
    return [p_ref[pl.ds(jj * tall + shifts[jj], rows), :] for jj in range(ranks)]


def filter_kernel(off_ref, wi_ref, lw_ref, g_ref, u_ref, mine_ref, other_ref, w_ref, band_ref, p_ref):
    ranks, segs, comps, total, width = g_ref.shape
    rows = total // ranks
    scale = 1.0 / (segs * 2)
    core = lax.axis_index("seg")
    fill_bands(u_ref, band_ref)
    for s in range(segs):
        for c in range(comps):
            for j in range(ranks):
                w_ref[s, c, j, :total] = g_ref[j, s, c]
                w_ref[s, c, j, total:] = g_ref[j, s, c, : rows + PAD]
            x = g_ref[0, s, c].astype(F32)
            x = jnp.concatenate([x[1:], x[:1]], 0).astype(BF16)
            w_ref[s, c, ranks, :total] = x
            w_ref[s, c, ranks, total:] = x[: rows + PAD]
    half = mine_ref.shape[0]
    weights = [lw_ref[wi_ref[s]] * scale for s in range(segs)]
    for out_ref, first in ((other_ref, (1 - core) * half), (mine_ref, core * half)):

        @pl.loop(0, half)
        def _(i):
            sums = None
            for s in range(segs):
                got = filter_one(w_ref, band_ref, p_ref.at[s], off_ref, s, first + i, rows, ranks)
                got = [weights[s] * x for x in got]
                sums = got if sums is None else [x + y for x, y in zip(sums, got)]
            for jj in range(ranks):
                out_ref[i, :, jj * BLOCK : (jj + 1) * BLOCK] = sums[jj].astype(out_ref.dtype)


def reversed_taps(kernels):
    k = kernels.astype(F32)
    zeros = jnp.zeros(k.shape[:-1] + (k.shape[-1],), F32)
    return jnp.concatenate([k[..., :1], zeros, jnp.flip(k[..., 1:], -1)], -1)


def params(**more):
    return pltpu.CompilerParams(vmem_limit_bytes=60 << 20, **more)


def body(samples, kernels, offsets, weight_index, level_weights):
    segs, comps, rows, cols = samples.shape
    ranks = lax.axis_size("freq")
    size_one = rows * ranks
    if cols != ranks * BLOCK or rows != BLOCK or lax.axis_size("seg") != 2:
        return general(samples, kernels, offsets, weight_index, level_weights)
    length = size_one * cols
    bins = np.arange(cols) - BLOCK // 2
    near = unit(np.arange(rows)[:, None] * bins[None, :] % length / length, 1.0 / math.sqrt(length))
    far = unit(np.arange(ranks)[:, None] * rows * bins[None, :] % length / length)
    turned = pl.pallas_call(
        first_kernel,
        out_shape=jax.ShapeDtypeStruct((ranks, segs, comps, rows, BLOCK), BF16),
        in_specs=[VMEM] * 9,
        out_specs=VMEM,
        scratch_shapes=[pltpu.VMEM((cols, cols), BF16)] * 2 + [pltpu.VMEM((segs * comps * rows, cols), BF16), pltpu.VMEM((16, cols), F32)],
        compiler_params=params(),
    )(samples, *wave_bases(cols, -(BLOCK // 2)), *near, *far)
    arrived = lax.all_to_all(turned, "freq", split_axis=0, concat_axis=0, tiled=True)
    spectrum = pl.pallas_call(
        second_kernel,
        out_shape=jax.ShapeDtypeStruct((segs, comps, size_one, BLOCK), BF16),
        in_specs=[VMEM] * 5,
        out_specs=VMEM,
        scratch_shapes=[pltpu.VMEM((size_one, size_one), BF16)] * 2
        + [pltpu.VMEM((size_one, segs * comps * BLOCK), BF16)],
        compiler_params=params(),
    )(arrived, *wave_bases(size_one, 0))
    gathered = lax.all_gather(spectrum, "freq", axis=0)
    half = kernels.shape[1] // 2
    tall = rows + PAD
    mine, other = pl.pallas_call(
        filter_kernel,
        out_shape=(
            jax.ShapeDtypeStruct((half, rows, cols), F32),
            jax.ShapeDtypeStruct((half, rows, cols), BF16),
        ),
        in_specs=[SMEM] * 3 + [VMEM] * 2,
        out_specs=(VMEM, VMEM),
        scratch_shapes=[
            pltpu.VMEM((segs, comps, ranks + 1, size_one + tall, BLOCK), BF16),
            pltpu.VMEM((kernels.shape[1], 4 * BLOCK, 2 * BLOCK), BF16),
            pltpu.VMEM((segs, ranks * tall, BLOCK), F32),
        ],
        compiler_params=params(),
    )(offsets, weight_index, level_weights, gathered, reversed_taps(kernels))
    swapped = lax.ppermute(other, "seg", [(0, 1), (1, 0)])
    return (mine + swapped.astype(F32)).reshape(half, rows * cols)


def solution(mesh):
    in_specs = (
        P(("parts", "seg"), None, "freq", None),
        P(),
        P(("parts", "seg"), None),
        P(("parts", "seg")),
        P(),
    )
    out_specs = P(("parts", "seg"), "freq")
    return jax.shard_map(body, mesh=mesh, in_specs=in_specs, out_specs=out_specs, check_vma=False)
```

```python
import math

import functools

import jax
import jax.numpy as jnp
import numpy as np
from jax import lax
from jax.experimental import pallas as pl
from jax.experimental.pallas import tpu as pltpu
from jax.sharding import PartitionSpec as P

BLOCK = 128
KERNELS = 8
REACH = 4
ROUTE_CAP = 4


def extended(cells, sides, width):
    for axis, dim in sides:
        count = lax.axis_size(axis)
        head = lax.slice_in_dim(cells, 0, width, axis=dim)
        tail = lax.slice_in_dim(cells, cells.shape[dim] - width, cells.shape[dim], axis=dim)
        cells = jnp.concatenate(
            [
                lax.ppermute(tail, axis, [(i, (i + 1) % count) for i in range(count)]),
                cells,
                lax.ppermute(head, axis, [((i + 1) % count, i) for i in range(count)]),
            ],
            axis=dim,
        )
    return cells


def passed_along(block, axis, distance):
    devices = range(lax.axis_size(axis))
    route = [((i - distance) % len(devices), i) for i in devices]
    return lax.ppermute(block, axis, route)


def dft_table(size):
    rows = lax.broadcasted_iota(jnp.int32, (size, size), 0)
    cols = lax.broadcasted_iota(jnp.int32, (size, size), 1)
    angle = (rows * cols % size).astype(jnp.float32) * (2.0 * math.pi / size)
    return (jnp.cos(angle), jnp.sin(angle))


def toeplitz(kernels):
    width = kernels.shape[-1]
    tail = jnp.zeros(kernels.shape[:-1] + (width + 1,), kernels.dtype)
    padded = jnp.concatenate([kernels, tail], -1)
    tiled = jnp.tile(padded, (1, 1, width))[..., : 2 * width * width]
    return tiled.reshape(kernels.shape[:-1] + (width, 2 * width))


def take_blocks(joined, start):
    return lax.dynamic_slice_in_dim(joined, start, joined.shape[0] // 2, 0)


def slide(joined, starts):
    return jax.vmap(jax.vmap(take_blocks))(joined, starts)


def general(samples, kernels, offsets, weight_index, level_weights):
    segs, comps, rows_one, cols_two = samples.shape
    ranks = lax.axis_size("freq")
    here = lax.axis_index("freq")
    size_one = rows_one * ranks
    length = size_one * cols_two
    highest = lax.Precision.HIGHEST
    cos_two, sin_two = dft_table(cols_two)
    stacked = samples.reshape(segs * comps * rows_one, cols_two)
    with_cos = jnp.dot(stacked, cos_two, precision=highest).reshape(samples.shape)
    with_sin = jnp.dot(stacked, sin_two, precision=highest).reshape(samples.shape)
    first_real = with_cos[:, 0] + with_sin[:, 1]
    first_imag = with_cos[:, 1] - with_sin[:, 0]
    row_global = here * rows_one + lax.broadcasted_iota(jnp.int32, (rows_one, cols_two), 0)
    col_global = lax.broadcasted_iota(jnp.int32, (rows_one, cols_two), 1)
    twist = (row_global * col_global % length).astype(jnp.float32) * (2.0 * math.pi / length)
    twist_cos = jnp.cos(twist)
    twist_sin = jnp.sin(twist)
    turned = jnp.stack(
        [
            first_real * twist_cos + first_imag * twist_sin,
            first_imag * twist_cos - first_real * twist_sin,
        ],
        1,
    )
    columns = lax.all_to_all(
        turned.astype(jnp.bfloat16), "freq", split_axis=3, concat_axis=3, tiled=True
    ).astype(turned.dtype)
    width_two = cols_two // ranks
    ordered = columns.reshape(segs, comps, rows_one, ranks, width_two)
    cos_one, sin_one = dft_table(size_one)
    cos_one = cos_one.reshape(ranks, rows_one, size_one)
    sin_one = sin_one.reshape(ranks, rows_one, size_one)
    second_cos = jnp.einsum("scirl,rik->sclk", ordered, cos_one, precision=highest)
    second_sin = jnp.einsum("scirl,rik->sclk", ordered, sin_one, precision=highest)
    second = jnp.stack(
        [second_cos[:, 0] + second_sin[:, 1], second_cos[:, 1] - second_sin[:, 0]], 1
    )
    arrived = lax.all_to_all(
        second.astype(jnp.bfloat16), "freq", split_axis=3, concat_axis=3, tiled=True
    ).astype(second.dtype)
    width_one = size_one // ranks
    spectrum = arrived.reshape(segs, comps, width_two, ranks, width_one)
    spectrum = jnp.transpose(spectrum, (0, 1, 4, 3, 2)).reshape(segs, comps, width_one * cols_two)
    spectrum = (spectrum * (1.0 / math.sqrt(length))).astype(jnp.bfloat16)
    half = BLOCK // 2
    edged = extended(spectrum, (("freq", 2),), half)
    bins_here = spectrum.shape[2]
    count = bins_here // BLOCK
    lower = edged[..., :bins_here].reshape(segs, comps, count, BLOCK)
    upper = edged[..., BLOCK:].reshape(segs, comps, count, BLOCK)
    window = jnp.concatenate([lower, upper], -1)
    bands = toeplitz(kernels)
    real_band = bands[0]
    imag_band = bands[1]
    table = jnp.stack(
        [jnp.stack([real_band, imag_band], 0), jnp.stack([-imag_band, real_band], 0)], 0
    )
    filtered = jnp.einsum("scbm,cokim->skboi", window, table, preferred_element_type=jnp.float32)
    power = (filtered[:, :, :, 0] ** 2 + filtered[:, :, :, 1] ** 2).astype(jnp.bfloat16)
    quotient = jnp.floor_divide(offsets, count)
    remainder = offsets - quotient * count
    following = passed_along(power, "freq", -1)
    inner = slide(jnp.concatenate([power, following], 2), remainder)
    plane_count = segs * KERNELS
    flat = inner.reshape(plane_count, count * BLOCK)
    plane_quot = quotient.reshape(plane_count)
    distances = lax.broadcasted_iota(jnp.int32, (2 * REACH + 1, plane_count), 0) - REACH
    member = (plane_quot[None, :] == distances).astype(jnp.int32)
    place = jnp.cumsum(member, 1) - 1
    slot_ids = lax.broadcasted_iota(jnp.int32, (2 * REACH + 1, ROUTE_CAP, plane_count), 1)
    select = ((member[:, None, :] == 1) & (place[:, None, :] == slot_ids)).astype(jnp.bfloat16)
    packed = jnp.einsum("dcp,pl->dcl", select, flat, preferred_element_type=jnp.float32).astype(
        jnp.bfloat16
    )
    received = []
    for step_index in range(2 * REACH + 1):
        received.append(passed_along(packed[step_index], "freq", -(step_index - REACH)))
    gathered = jnp.stack(received, 0)
    placed = jnp.einsum("dcp,dcl->pl", select, gathered, preferred_element_type=jnp.float32)
    shifted = placed.astype(jnp.bfloat16).reshape(segs, KERNELS, count, BLOCK)
    levels = lax.broadcasted_iota(jnp.int32, (segs, level_weights.shape[0]), 1)
    weights = jnp.sum(jnp.where(weight_index[:, None] == levels, level_weights[None, :], 0.0), 1)
    scale = 1.0 / (segs * lax.axis_size("seg"))
    partial_sum = jnp.sum((weights * scale)[:, None, None, None] * shifted.astype(jnp.float32), 0)
    owned = lax.psum_scatter(
        partial_sum.astype(jnp.bfloat16), "seg", scatter_dimension=0, tiled=True
    ).astype(jnp.float32)
    return owned.reshape(owned.shape[0], count * BLOCK)


VMEM = pl.BlockSpec(memory_space=pltpu.VMEM)
SMEM = pl.BlockSpec(memory_space=pltpu.SMEM)
PAD = 16
BF16 = jnp.bfloat16
F32 = jnp.float32


def unit(turns, scale=1.0):
    angle = 2.0 * np.pi * turns
    return (np.cos(angle) * scale).astype(np.float32), (np.sin(angle) * scale).astype(np.float32)


def wave_bases(size, first):
    step = math.isqrt(size)
    while size % step:
        step -= 1
    cols = np.arange(size) + first
    low = np.arange(step)[:, None] * cols[None, :] % size / size
    high = np.arange(size // step)[:, None] * step * cols[None, :] % size / size
    return unit(low) + unit(high)


def fill_waves(low_cos, low_sin, high_cos, high_sin, cos_ref, sin_ref):
    step = low_cos.shape[0]

    @pl.loop(0, high_cos.shape[0])
    def _(i):
        hc = high_cos[pl.ds(i, 1), :]
        hs = high_sin[pl.ds(i, 1), :]
        lc = low_cos[...]
        ls = low_sin[...]
        rows = pl.ds(pl.multiple_of(i * step, step), step)
        cos_ref[rows, :] = (hc * lc - hs * ls).astype(BF16)
        sin_ref[rows, :] = (hs * lc + hc * ls).astype(BF16)


def fill_bands(u_ref, band_ref):
    wide = 2 * BLOCK

    @pl.loop(0, u_ref.shape[1])
    def _(t):
        both = []
        for c in range(2):
            row = jnp.broadcast_to(u_ref[c, pl.ds(t, 1), :], (wide, wide))
            both.append(pltpu.roll(row, 0, 1, stride=1, stride_axis=0)[:, :BLOCK])
        re, im = both
        band_ref[t, :wide, :BLOCK] = re.astype(BF16)
        band_ref[t, :wide, BLOCK:] = im.astype(BF16)
        band_ref[t, wide:, :BLOCK] = (-im).astype(BF16)
        band_ref[t, wide:, BLOCK:] = re.astype(BF16)


def remote(src, dst, sems, at, axis, device):
    return pltpu.make_async_remote_copy(
        src_ref=src,
        dst_ref=dst,
        send_sem=sems[0].at[at],
        recv_sem=sems[1].at[at],
        device_id={axis: device},
        device_id_type=pl.DeviceIdType.MESH,
    )


def first_step(s, x_ref, cos_ref, sin_ref, xb_ref, near_cos, near_sin, far_ref, j):
    rows = x_ref.shape[2]
    lanes = pl.ds(pl.multiple_of(j * BLOCK, BLOCK), BLOCK)
    rhs = jnp.concatenate([cos_ref[:, lanes], sin_ref[:, lanes]], 1)
    got = jnp.dot(xb_ref[s], rhs, preferred_element_type=F32)
    a = far_ref[0:1, lanes]
    b = far_ref[8:9, lanes]
    wc = a * near_cos[:, lanes] - b * near_sin[:, lanes]
    ws = b * near_cos[:, lanes] + a * near_sin[:, lanes]
    re = got[:rows, :BLOCK] + got[rows:, BLOCK:]
    im = got[rows:, :BLOCK] - got[:rows, BLOCK:]
    return jnp.concatenate([re * wc + im * ws, im * wc - re * ws], 1).astype(BF16)


def second_step(s, cos_ref, sin_ref, rhs_ref, w_ref, me, ranks):
    rows = cos_ref.shape[0] // ranks

    @pl.loop(0, ranks)
    def _(i):
        here = pl.ds(pl.multiple_of(i * rows, rows), rows)
        yc = jnp.dot(cos_ref[here, :], rhs_ref[s], preferred_element_type=F32)
        ys = jnp.dot(sin_ref[here, :], rhs_ref[s], preferred_element_type=F32)
        w_ref[0, me, here, :] = (yc[:, :BLOCK] + ys[:, BLOCK:]).astype(BF16)
        w_ref[1, me, here, :] = (yc[:, BLOCK:] - ys[:, :BLOCK]).astype(BF16)


def pad_edges(w_ref, total, ranks):
    tall = w_ref.shape[2] - total
    for c in range(2):
        x = w_ref[c, 0, :total, :].astype(F32)
        w_ref[c, ranks, :total, :] = jnp.concatenate([x[1:], x[:1]], 0).astype(BF16)
        for j in range(ranks + 1):
            w_ref[c, j, total:, :] = w_ref[c, j, :tall, :]


def filter_one(w_ref, band_ref, p_ref, off_ref, s, t, rows, ranks):
    total = rows * ranks
    here = lax.axis_index("freq")
    blocks = total * ranks
    base = lax.rem(here * total + off_ref[s, t] + blocks, blocks)
    gk = base // ranks
    gj = base - gk * ranks
    tall = rows + PAD
    parts = []
    shifts = []
    for jj in range(ranks):
        carry = (gj + jj) // ranks
        j = gj + jj - carry * ranks
        row = lax.rem(gk + carry, total)
        low = row // PAD * PAD
        shifts.append(row - low)
        take = pl.ds(pl.multiple_of(low, PAD), tall)
        pieces = [w_ref[0, j, take, :], w_ref[0, j + 1, take, :], w_ref[1, j, take, :], w_ref[1, j + 1, take, :]]
        parts.append(jnp.concatenate(pieces, 1))
    got = jnp.dot(jnp.concatenate(parts, 0), band_ref[t], preferred_element_type=F32)
    re = got[:, :BLOCK]
    im = got[:, BLOCK:]
    p_ref[...] = re * re + im * im
    return [p_ref[pl.ds(jj * tall + shifts[jj], rows), :] for jj in range(ranks)]


def gather_kernel(
    x_ref, u_ref,
    b_lc, b_ls, b_hc, b_hs, e_lc, e_ls, e_hc, e_hs, near_cos, near_sin, far_cos, far_sin,
    w_first, w_second, band_ref,
    cos_ref, sin_ref, xb_ref, far_ref, turned, rhs_ref,
    ex_send, ex_recv, up_send, up_recv, down_send, down_recv,
):
    segs, comps, rows, cols = x_ref.shape
    ranks = lax.axis_size("freq")
    total = rows * ranks
    me = lax.axis_index("freq")
    w_refs = (w_first, w_second)
    exchange = (ex_send, ex_recv)

    barrier = pltpu.get_barrier_semaphore()
    for d in range(1, ranks):
        peer = (me + d) % ranks
        pl.semaphore_signal(barrier, inc=1, device_id={"freq": peer}, device_id_type=pl.DeviceIdType.MESH)
    pl.semaphore_wait(barrier, ranks - 1)

    fill_waves(b_lc, b_ls, b_hc, b_hs, cos_ref, sin_ref)
    far_ref[0:1, :] = far_cos[pl.ds(me, 1), :]
    far_ref[8:9, :] = far_sin[pl.ds(me, 1), :]
    for s in range(segs):
        for c in range(comps):
            xb_ref[s, c * rows : (c + 1) * rows, :] = x_ref[s, c].astype(BF16)

    def sent(s, d):
        here = pl.ds(pl.multiple_of(me * rows, rows), rows)
        return remote(turned.at[s, d], rhs_ref.at[s, here, :], exchange, (s, d), "freq", (me + d) % ranks)

    def own_rows():
        return pl.ds(pl.multiple_of(me * rows, rows), rows)

    for s in range(segs):
        step = functools.partial(first_step, s, x_ref, cos_ref, sin_ref, xb_ref, near_cos, near_sin, far_ref)

        @pl.loop(1, ranks)
        def _(d):
            turned[s, d] = step((me + d) % ranks)
            sent(s, d).start()

        rhs_ref[s, own_rows(), :] = step(me)

    fill_waves(e_lc, e_ls, e_hc, e_hs, cos_ref, sin_ref)
    fill_bands(u_ref, band_ref)

    odd = me % 2
    place = (1 - odd) * (me // 2) + odd * (ranks - 1 - me // 2)

    def at_place(p):
        p = (p + ranks) % ranks
        far = p // (ranks // 2)
        return (1 - far) * (2 * p) + far * (2 * (ranks - 1 - p) + 1)

    mid = total // 2

    def hop(s, c, k, way):
        owner = at_place(place - k) if way == 0 else at_place(place + k)
        target = at_place(place + 1) if way == 0 else at_place(place - 1)
        block = w_refs[s].at[c, owner, pl.ds(way * mid, mid), :]
        sems = ((up_send, up_recv), (down_send, down_recv))[way]
        return remote(block, block, sems, (s, c, k), "freq", target)

    def landed(s, c, k, way):
        owner = at_place(place - k - 1) if way == 0 else at_place(place + k + 1)
        target = at_place(place + 1) if way == 0 else at_place(place - 1)
        block = w_refs[s].at[c, owner, pl.ds(way * mid, mid), :]
        sems = ((up_send, up_recv), (down_send, down_recv))[way]
        return remote(block, block, sems, (s, c, k), "freq", target)

    for s in range(segs):
        for d in range(1, ranks):
            here = pl.ds(pl.multiple_of((me + ranks - d) % ranks * rows, rows), rows)
            remote(turned.at[s, d], rhs_ref.at[s, here, :], exchange, (s, d), "freq", (me + d) % ranks).wait_recv()
        second_step(s, cos_ref, sin_ref, rhs_ref, w_refs[s], me, ranks)
        for c in range(comps):
            for way in range(2):
                hop(s, c, 0, way).start()

    def advance(s, k):
        for c in range(comps):
            for way in range(2):
                landed(s, c, k - 1, way).wait_recv()
                if k < ranks - 1:
                    hop(s, c, k, way).start()

    for s in range(segs):
        for k in range(1, ranks):
            advance(s, k)
        pad_edges(w_refs[s], total, ranks)

    for s in range(segs):
        for d in range(1, ranks):
            sent(s, d).wait_send()
        for c in range(comps):
            for k in range(ranks - 1):
                for way in range(2):
                    hop(s, c, k, way).wait_send()


def filter_kernel(off_ref, wi_ref, lw_ref, w_first, w_second, band_ref, mine_ref, other_ref, p_ref):
    half, rows, cols = mine_ref.shape
    ranks = cols // BLOCK
    w_refs = (w_first, w_second)
    scale = 1.0 / (2 * len(w_refs))
    core = lax.axis_index("seg")
    weights = [lw_ref[wi_ref[s]] * scale for s in range(len(w_refs))]
    for out_ref, first in ((other_ref, (1 - core) * half), (mine_ref, core * half)):

        @pl.loop(0, half)
        def _(i):
            sums = None
            for s, w_ref in enumerate(w_refs):
                got = filter_one(w_ref, band_ref, p_ref.at[s], off_ref, s, first + i, rows, ranks)
                got = [weights[s] * x for x in got]
                sums = got if sums is None else [x + y for x, y in zip(sums, got)]
            for jj in range(ranks):
                out_ref[i, :, jj * BLOCK : (jj + 1) * BLOCK] = sums[jj].astype(out_ref.dtype)


def reversed_taps(kernels):
    k = kernels.astype(F32)
    zeros = jnp.zeros(k.shape[:-1] + (k.shape[-1],), F32)
    return jnp.concatenate([k[..., :1], zeros, jnp.flip(k[..., 1:], -1)], -1)


def body(samples, kernels, offsets, weight_index, level_weights):
    segs, comps, rows, cols = samples.shape
    ranks = lax.axis_size("freq")
    size_one = rows * ranks
    if cols != ranks * BLOCK or rows != BLOCK or size_one != cols or segs != 2 or lax.axis_size("seg") != 2:
        return general(samples, kernels, offsets, weight_index, level_weights)
    length = size_one * cols
    bins = np.arange(cols) - BLOCK // 2
    near = unit(np.arange(rows)[:, None] * bins[None, :] % length / length, 1.0 / math.sqrt(length))
    far = unit(np.arange(ranks)[:, None] * rows * bins[None, :] % length / length)
    half = kernels.shape[1] // 2
    tall = rows + PAD
    copies = pltpu.SemaphoreType.DMA
    gathered = jax.ShapeDtypeStruct((comps, ranks + 1, size_one + tall, BLOCK), BF16)
    bands = jax.ShapeDtypeStruct((kernels.shape[1], 4 * BLOCK, 2 * BLOCK), BF16)
    first, second, bands = pl.pallas_call(
        gather_kernel,
        out_shape=(gathered, gathered, bands),
        in_specs=[VMEM] * 14,
        out_specs=(VMEM, VMEM, VMEM),
        scratch_shapes=[pltpu.VMEM((cols, cols), BF16)] * 2
        + [
            pltpu.VMEM((segs, comps * rows, cols), BF16),
            pltpu.VMEM((16, cols), F32),
            pltpu.VMEM((segs, ranks, rows, 2 * BLOCK), BF16),
            pltpu.VMEM((segs, size_one, 2 * BLOCK), BF16),
        ]
        + [copies((segs, ranks))] * 2
        + [copies((segs, comps, ranks - 1))] * 4,
        compiler_params=pltpu.CompilerParams(vmem_limit_bytes=36 << 20, collective_id=0, has_side_effects=True),
    )(
        samples, reversed_taps(kernels),
        *wave_bases(cols, -(BLOCK // 2)), *wave_bases(size_one, 0), *near, *far,
    )
    mine, other = pl.pallas_call(
        filter_kernel,
        out_shape=(
            jax.ShapeDtypeStruct((half, rows, cols), F32),
            jax.ShapeDtypeStruct((half, rows, cols), BF16),
        ),
        in_specs=[SMEM] * 3 + [VMEM] * 3,
        out_specs=(VMEM, VMEM),
        scratch_shapes=[pltpu.VMEM((segs, ranks * tall, BLOCK), F32)],
        compiler_params=pltpu.CompilerParams(vmem_limit_bytes=28 << 20),
    )(offsets, weight_index, level_weights, first, second, bands)
    swapped = lax.ppermute(other, "seg", [(0, 1), (1, 0)])
    return (mine + swapped.astype(F32)).reshape(half, rows * cols)


def solution(mesh):
    in_specs = (
        P(("parts", "seg"), None, "freq", None),
        P(),
        P(("parts", "seg"), None),
        P(("parts", "seg")),
        P(),
    )
    out_specs = P(("parts", "seg"), "freq")
    return jax.shard_map(body, mesh=mesh, in_specs=in_specs, out_specs=out_specs, check_vma=False)
```

```python
import math

import functools

import jax
import jax.numpy as jnp
import numpy as np
from jax import lax
from jax.experimental import pallas as pl
from jax.experimental.pallas import tpu as pltpu
from jax.sharding import PartitionSpec as P

BLOCK = 128
KERNELS = 8
REACH = 4
ROUTE_CAP = 4


def extended(cells, sides, width):
    for axis, dim in sides:
        count = lax.axis_size(axis)
        head = lax.slice_in_dim(cells, 0, width, axis=dim)
        tail = lax.slice_in_dim(cells, cells.shape[dim] - width, cells.shape[dim], axis=dim)
        cells = jnp.concatenate(
            [
                lax.ppermute(tail, axis, [(i, (i + 1) % count) for i in range(count)]),
                cells,
                lax.ppermute(head, axis, [((i + 1) % count, i) for i in range(count)]),
            ],
            axis=dim,
        )
    return cells


def passed_along(block, axis, distance):
    devices = range(lax.axis_size(axis))
    route = [((i - distance) % len(devices), i) for i in devices]
    return lax.ppermute(block, axis, route)


def dft_table(size):
    rows = lax.broadcasted_iota(jnp.int32, (size, size), 0)
    cols = lax.broadcasted_iota(jnp.int32, (size, size), 1)
    angle = (rows * cols % size).astype(jnp.float32) * (2.0 * math.pi / size)
    return (jnp.cos(angle), jnp.sin(angle))


def toeplitz(kernels):
    width = kernels.shape[-1]
    tail = jnp.zeros(kernels.shape[:-1] + (width + 1,), kernels.dtype)
    padded = jnp.concatenate([kernels, tail], -1)
    tiled = jnp.tile(padded, (1, 1, width))[..., : 2 * width * width]
    return tiled.reshape(kernels.shape[:-1] + (width, 2 * width))


def take_blocks(joined, start):
    return lax.dynamic_slice_in_dim(joined, start, joined.shape[0] // 2, 0)


def slide(joined, starts):
    return jax.vmap(jax.vmap(take_blocks))(joined, starts)


def general(samples, kernels, offsets, weight_index, level_weights):
    segs, comps, rows_one, cols_two = samples.shape
    ranks = lax.axis_size("freq")
    here = lax.axis_index("freq")
    size_one = rows_one * ranks
    length = size_one * cols_two
    highest = lax.Precision.HIGHEST
    cos_two, sin_two = dft_table(cols_two)
    stacked = samples.reshape(segs * comps * rows_one, cols_two)
    with_cos = jnp.dot(stacked, cos_two, precision=highest).reshape(samples.shape)
    with_sin = jnp.dot(stacked, sin_two, precision=highest).reshape(samples.shape)
    first_real = with_cos[:, 0] + with_sin[:, 1]
    first_imag = with_cos[:, 1] - with_sin[:, 0]
    row_global = here * rows_one + lax.broadcasted_iota(jnp.int32, (rows_one, cols_two), 0)
    col_global = lax.broadcasted_iota(jnp.int32, (rows_one, cols_two), 1)
    twist = (row_global * col_global % length).astype(jnp.float32) * (2.0 * math.pi / length)
    twist_cos = jnp.cos(twist)
    twist_sin = jnp.sin(twist)
    turned = jnp.stack(
        [
            first_real * twist_cos + first_imag * twist_sin,
            first_imag * twist_cos - first_real * twist_sin,
        ],
        1,
    )
    columns = lax.all_to_all(
        turned.astype(jnp.bfloat16), "freq", split_axis=3, concat_axis=3, tiled=True
    ).astype(turned.dtype)
    width_two = cols_two // ranks
    ordered = columns.reshape(segs, comps, rows_one, ranks, width_two)
    cos_one, sin_one = dft_table(size_one)
    cos_one = cos_one.reshape(ranks, rows_one, size_one)
    sin_one = sin_one.reshape(ranks, rows_one, size_one)
    second_cos = jnp.einsum("scirl,rik->sclk", ordered, cos_one, precision=highest)
    second_sin = jnp.einsum("scirl,rik->sclk", ordered, sin_one, precision=highest)
    second = jnp.stack(
        [second_cos[:, 0] + second_sin[:, 1], second_cos[:, 1] - second_sin[:, 0]], 1
    )
    arrived = lax.all_to_all(
        second.astype(jnp.bfloat16), "freq", split_axis=3, concat_axis=3, tiled=True
    ).astype(second.dtype)
    width_one = size_one // ranks
    spectrum = arrived.reshape(segs, comps, width_two, ranks, width_one)
    spectrum = jnp.transpose(spectrum, (0, 1, 4, 3, 2)).reshape(segs, comps, width_one * cols_two)
    spectrum = (spectrum * (1.0 / math.sqrt(length))).astype(jnp.bfloat16)
    half = BLOCK // 2
    edged = extended(spectrum, (("freq", 2),), half)
    bins_here = spectrum.shape[2]
    count = bins_here // BLOCK
    lower = edged[..., :bins_here].reshape(segs, comps, count, BLOCK)
    upper = edged[..., BLOCK:].reshape(segs, comps, count, BLOCK)
    window = jnp.concatenate([lower, upper], -1)
    bands = toeplitz(kernels)
    real_band = bands[0]
    imag_band = bands[1]
    table = jnp.stack(
        [jnp.stack([real_band, imag_band], 0), jnp.stack([-imag_band, real_band], 0)], 0
    )
    filtered = jnp.einsum("scbm,cokim->skboi", window, table, preferred_element_type=jnp.float32)
    power = (filtered[:, :, :, 0] ** 2 + filtered[:, :, :, 1] ** 2).astype(jnp.bfloat16)
    quotient = jnp.floor_divide(offsets, count)
    remainder = offsets - quotient * count
    following = passed_along(power, "freq", -1)
    inner = slide(jnp.concatenate([power, following], 2), remainder)
    plane_count = segs * KERNELS
    flat = inner.reshape(plane_count, count * BLOCK)
    plane_quot = quotient.reshape(plane_count)
    distances = lax.broadcasted_iota(jnp.int32, (2 * REACH + 1, plane_count), 0) - REACH
    member = (plane_quot[None, :] == distances).astype(jnp.int32)
    place = jnp.cumsum(member, 1) - 1
    slot_ids = lax.broadcasted_iota(jnp.int32, (2 * REACH + 1, ROUTE_CAP, plane_count), 1)
    select = ((member[:, None, :] == 1) & (place[:, None, :] == slot_ids)).astype(jnp.bfloat16)
    packed = jnp.einsum("dcp,pl->dcl", select, flat, preferred_element_type=jnp.float32).astype(
        jnp.bfloat16
    )
    received = []
    for step_index in range(2 * REACH + 1):
        received.append(passed_along(packed[step_index], "freq", -(step_index - REACH)))
    gathered = jnp.stack(received, 0)
    placed = jnp.einsum("dcp,dcl->pl", select, gathered, preferred_element_type=jnp.float32)
    shifted = placed.astype(jnp.bfloat16).reshape(segs, KERNELS, count, BLOCK)
    levels = lax.broadcasted_iota(jnp.int32, (segs, level_weights.shape[0]), 1)
    weights = jnp.sum(jnp.where(weight_index[:, None] == levels, level_weights[None, :], 0.0), 1)
    scale = 1.0 / (segs * lax.axis_size("seg"))
    partial_sum = jnp.sum((weights * scale)[:, None, None, None] * shifted.astype(jnp.float32), 0)
    owned = lax.psum_scatter(
        partial_sum.astype(jnp.bfloat16), "seg", scatter_dimension=0, tiled=True
    ).astype(jnp.float32)
    return owned.reshape(owned.shape[0], count * BLOCK)


VMEM = pl.BlockSpec(memory_space=pltpu.VMEM)
SMEM = pl.BlockSpec(memory_space=pltpu.SMEM)
PAD = 16
BF16 = jnp.bfloat16
F32 = jnp.float32


def unit(turns, scale=1.0):
    angle = 2.0 * np.pi * turns
    return (np.cos(angle) * scale).astype(np.float32), (np.sin(angle) * scale).astype(np.float32)


def wave_bases(size, first):
    step = math.isqrt(size)
    while size % step:
        step -= 1
    cols = np.arange(size) + first
    low = np.arange(step)[:, None] * cols[None, :] % size / size
    high = np.arange(size // step)[:, None] * step * cols[None, :] % size / size
    return unit(low) + unit(high)


def fill_waves(low_cos, low_sin, high_cos, high_sin, cos_ref, sin_ref):
    step = low_cos.shape[0]

    @pl.loop(0, high_cos.shape[0])
    def _(i):
        hc = high_cos[pl.ds(i, 1), :]
        hs = high_sin[pl.ds(i, 1), :]
        lc = low_cos[...]
        ls = low_sin[...]
        rows = pl.ds(pl.multiple_of(i * step, step), step)
        cos_ref[rows, :] = (hc * lc - hs * ls).astype(BF16)
        sin_ref[rows, :] = (hs * lc + hc * ls).astype(BF16)


def fill_bands(taps_ref, band_ref):
    wide = 2 * BLOCK
    for t in range(taps_ref.shape[1]):
        both = []
        for c in range(2):
            row = taps_ref[c, t : t + 1, :].astype(F32)
            row = jnp.concatenate([row, jnp.zeros_like(row)], 1)
            row = jnp.broadcast_to(row, (BLOCK, wide))
            both.append(pltpu.roll(row, 0, 1, stride=1, stride_axis=0).T)
        re, im = both
        band_ref[t, :wide, :BLOCK] = re.astype(BF16)
        band_ref[t, :wide, BLOCK:] = im.astype(BF16)
        band_ref[t, wide:, :BLOCK] = (-im).astype(BF16)
        band_ref[t, wide:, BLOCK:] = re.astype(BF16)


def remote(src, dst, sems, at, axis, device):
    return pltpu.make_async_remote_copy(
        src_ref=src,
        dst_ref=dst,
        send_sem=sems[0].at[at],
        recv_sem=sems[1].at[at],
        device_id={axis: device},
        device_id_type=pl.DeviceIdType.MESH,
    )


def first_step(s, x_ref, cos_ref, sin_ref, xb_ref, near_cos, near_sin, far_ref, j):
    rows = x_ref.shape[2]
    lanes = pl.ds(pl.multiple_of(j * BLOCK, BLOCK), BLOCK)
    rhs = jnp.concatenate([cos_ref[:, lanes], sin_ref[:, lanes]], 1)
    got = jnp.dot(xb_ref[s], rhs, preferred_element_type=F32)
    a = far_ref[0:1, lanes]
    b = far_ref[8:9, lanes]
    wc = a * near_cos[:, lanes] - b * near_sin[:, lanes]
    ws = b * near_cos[:, lanes] + a * near_sin[:, lanes]
    re = got[:rows, :BLOCK] + got[rows:, BLOCK:]
    im = got[rows:, :BLOCK] - got[:rows, BLOCK:]
    return jnp.concatenate([re * wc + im * ws, im * wc - re * ws], 1).astype(BF16)


def second_step(s, cos_ref, sin_ref, rhs_ref, w_ref, me, ranks):
    rows = cos_ref.shape[0] // ranks

    @pl.loop(0, ranks)
    def _(i):
        here = pl.ds(pl.multiple_of(i * rows, rows), rows)
        yc = jnp.dot(cos_ref[here, :], rhs_ref[s], preferred_element_type=F32)
        ys = jnp.dot(sin_ref[here, :], rhs_ref[s], preferred_element_type=F32)
        w_ref[0, me, here, :] = (yc[:, :BLOCK] + ys[:, BLOCK:]).astype(BF16)
        w_ref[1, me, here, :] = (yc[:, BLOCK:] - ys[:, :BLOCK]).astype(BF16)


def pad_edges(w_ref, total, ranks):
    tall = w_ref.shape[2] - total
    for c in range(2):
        x = w_ref[c, 0, :total, :].astype(F32)
        w_ref[c, ranks, :total, :] = jnp.concatenate([x[1:], x[:1]], 0).astype(BF16)
        for j in range(ranks + 1):
            w_ref[c, j, total:, :] = w_ref[c, j, :tall, :]


def filter_one(w_ref, band_ref, p_ref, off_ref, s, t, rows, ranks):
    total = rows * ranks
    here = lax.axis_index("freq")
    blocks = total * ranks
    base = lax.rem(here * total + off_ref[s, t] + blocks, blocks)
    gk = base // ranks
    gj = base - gk * ranks
    tall = rows + PAD
    parts = []
    shifts = []
    for jj in range(ranks):
        carry = (gj + jj) // ranks
        j = gj + jj - carry * ranks
        row = lax.rem(gk + carry, total)
        low = row // PAD * PAD
        shifts.append(row - low)
        take = pl.ds(pl.multiple_of(low, PAD), tall)
        pieces = [w_ref[0, j, take, :], w_ref[0, j + 1, take, :], w_ref[1, j, take, :], w_ref[1, j + 1, take, :]]
        parts.append(jnp.concatenate(pieces, 1))
    got = jnp.dot(jnp.concatenate(parts, 0), band_ref[t], preferred_element_type=F32)
    re = got[:, :BLOCK]
    im = got[:, BLOCK:]
    p_ref[...] = re * re + im * im
    return [p_ref[pl.ds(jj * tall + shifts[jj], rows), :] for jj in range(ranks)]


def gather_kernel(
    marks,
    x_ref, table_ref, taps_ref,
    w_first, w_second, band_ref,
    cos_ref, sin_ref, xb_ref, far_ref, turned, rhs_ref,
    ex_send, ex_recv, up_send, up_recv, down_send, down_recv,
):
    segs, comps, rows, cols = x_ref.shape
    ranks = lax.axis_size("freq")
    total = rows * ranks
    me = lax.axis_index("freq")
    w_refs = (w_first, w_second)
    exchange = (ex_send, ex_recv)

    tables = [table_ref.at[marks[i] : marks[i + 1], :] for i in range(len(marks) - 1)]
    b_lc, b_ls, b_hc, b_hs, e_lc, e_ls, e_hc, e_hs, near_cos, near_sin, far_cos, far_sin = tables
    barrier = pltpu.get_barrier_semaphore()
    for d in range(1, ranks):
        peer = (me + d) % ranks
        pl.semaphore_signal(barrier, inc=1, device_id={"freq": peer}, device_id_type=pl.DeviceIdType.MESH)
    pl.semaphore_wait(barrier, ranks - 1)

    fill_waves(b_lc, b_ls, b_hc, b_hs, cos_ref, sin_ref)
    far_ref[0:1, :] = far_cos[pl.ds(me, 1), :]
    far_ref[8:9, :] = far_sin[pl.ds(me, 1), :]
    for s in range(segs):
        for c in range(comps):
            xb_ref[s, c * rows : (c + 1) * rows, :] = x_ref[s, c].astype(BF16)

    def sent(s, d):
        here = pl.ds(pl.multiple_of(me * rows, rows), rows)
        return remote(turned.at[s, d], rhs_ref.at[s, here, :], exchange, (s, d), "freq", (me + d) % ranks)

    def own_rows():
        return pl.ds(pl.multiple_of(me * rows, rows), rows)

    for s in range(segs):
        step = functools.partial(first_step, s, x_ref, cos_ref, sin_ref, xb_ref, near_cos, near_sin, far_ref)

        @pl.loop(1, ranks)
        def _(d):
            turned[s, d] = step((me + d) % ranks)
            sent(s, d).start()

        rhs_ref[s, own_rows(), :] = step(me)

    fill_waves(e_lc, e_ls, e_hc, e_hs, cos_ref, sin_ref)
    fill_bands(taps_ref, band_ref)

    odd = me % 2
    place = (1 - odd) * (me // 2) + odd * (ranks - 1 - me // 2)

    def at_place(p):
        p = (p + ranks) % ranks
        far = p // (ranks // 2)
        return (1 - far) * (2 * p) + far * (2 * (ranks - 1 - p) + 1)

    mid = total // 2

    def hop(s, c, k, way):
        owner = at_place(place - k) if way == 0 else at_place(place + k)
        target = at_place(place + 1) if way == 0 else at_place(place - 1)
        block = w_refs[s].at[c, owner, pl.ds(way * mid, mid), :]
        sems = ((up_send, up_recv), (down_send, down_recv))[way]
        return remote(block, block, sems, (s, c, k), "freq", target)

    def landed(s, c, k, way):
        owner = at_place(place - k - 1) if way == 0 else at_place(place + k + 1)
        target = at_place(place + 1) if way == 0 else at_place(place - 1)
        block = w_refs[s].at[c, owner, pl.ds(way * mid, mid), :]
        sems = ((up_send, up_recv), (down_send, down_recv))[way]
        return remote(block, block, sems, (s, c, k), "freq", target)

    for s in range(segs):
        for d in range(1, ranks):
            here = pl.ds(pl.multiple_of((me + ranks - d) % ranks * rows, rows), rows)
            remote(turned.at[s, d], rhs_ref.at[s, here, :], exchange, (s, d), "freq", (me + d) % ranks).wait_recv()
        second_step(s, cos_ref, sin_ref, rhs_ref, w_refs[s], me, ranks)
        for c in range(comps):
            for way in range(2):
                hop(s, c, 0, way).start()

    def advance(s, k):
        for c in range(comps):
            for way in range(2):
                landed(s, c, k - 1, way).wait_recv()
                if k < ranks - 1:
                    hop(s, c, k, way).start()

    for k in range(1, ranks):
        for s in range(segs):
            advance(s, k)
    for s in range(segs):
        pad_edges(w_refs[s], total, ranks)

    for s in range(segs):
        for d in range(1, ranks):
            sent(s, d).wait_send()
        for c in range(comps):
            for k in range(ranks - 1):
                for way in range(2):
                    hop(s, c, k, way).wait_send()


def filter_kernel(own, off_ref, wi_ref, lw_ref, w_first, w_second, band_ref, out_ref, p_ref):
    half, rows, cols = out_ref.shape
    ranks = cols // BLOCK
    w_refs = (w_first, w_second)
    scale = 1.0 / (2 * len(w_refs))
    core = lax.axis_index("seg")
    weights = [lw_ref[wi_ref[s]] * scale for s in range(len(w_refs))]
    first = (core if own else 1 - core) * half

    @pl.loop(0, half)
    def _(i):
        sums = None
        for s, w_ref in enumerate(w_refs):
            got = filter_one(w_ref, band_ref, p_ref.at[s], off_ref, s, first + i, rows, ranks)
            got = [weights[s] * x for x in got]
            sums = got if sums is None else [x + y for x, y in zip(sums, got)]
        for jj in range(ranks):
            out_ref[i, :, jj * BLOCK : (jj + 1) * BLOCK] = sums[jj].astype(out_ref.dtype)


def body(samples, kernels, offsets, weight_index, level_weights):
    segs, comps, rows, cols = samples.shape
    ranks = lax.axis_size("freq")
    size_one = rows * ranks
    if cols != ranks * BLOCK or rows != BLOCK or size_one != cols or segs != 2 or lax.axis_size("seg") != 2:
        return general(samples, kernels, offsets, weight_index, level_weights)
    length = size_one * cols
    bins = np.arange(cols) - BLOCK // 2
    near = unit(np.arange(rows)[:, None] * bins[None, :] % length / length, 1.0 / math.sqrt(length))
    far = unit(np.arange(ranks)[:, None] * rows * bins[None, :] % length / length)
    half = kernels.shape[1] // 2
    tall = rows + PAD
    copies = pltpu.SemaphoreType.DMA
    gathered = jax.ShapeDtypeStruct((comps, ranks + 1, size_one + tall, BLOCK), BF16)
    bands = jax.ShapeDtypeStruct((kernels.shape[1], 4 * BLOCK, 2 * BLOCK), BF16)
    tables = (*wave_bases(cols, -(BLOCK // 2)), *wave_bases(size_one, 0), *near, *far)
    marks = np.cumsum([0] + [len(x) for x in tables]).tolist()
    first, second, bands = pl.pallas_call(
        functools.partial(gather_kernel, marks),
        out_shape=(gathered, gathered, bands),
        in_specs=[VMEM] * 3,
        out_specs=(VMEM, VMEM, VMEM),
        scratch_shapes=[pltpu.VMEM((cols, cols), BF16)] * 2
        + [
            pltpu.VMEM((segs, comps * rows, cols), BF16),
            pltpu.VMEM((16, cols), F32),
            pltpu.VMEM((segs, ranks, rows, 2 * BLOCK), BF16),
            pltpu.VMEM((segs, size_one, 2 * BLOCK), BF16),
        ]
        + [copies((segs, ranks))] * 2
        + [copies((segs, comps, ranks - 1))] * 4,
        compiler_params=pltpu.CompilerParams(vmem_limit_bytes=36 << 20, collective_id=0, has_side_effects=True),
    )(samples, np.concatenate(tables), kernels)

    def filtered(own, kind):
        flops = 2 * 8 * half * segs * ranks * tall * BLOCK * BLOCK
        return pl.pallas_call(
            functools.partial(filter_kernel, own),
            out_shape=jax.ShapeDtypeStruct((half, rows, cols), kind),
            in_specs=[SMEM] * 3 + [VMEM] * 3,
            out_specs=VMEM,
            scratch_shapes=[pltpu.VMEM((segs, ranks * tall, BLOCK), F32)],
            compiler_params=pltpu.CompilerParams(vmem_limit_bytes=24 << 20),
            cost_estimate=pl.CostEstimate(flops=flops, bytes_accessed=8 << 20, transcendentals=0),
        )(offsets, weight_index, level_weights, first, second, bands)

    swapped = lax.ppermute(filtered(False, BF16), "seg", [(0, 1), (1, 0)])
    return (filtered(True, F32) + swapped.astype(F32)).reshape(half, rows * cols)


def solution(mesh):
    in_specs = (
        P(("parts", "seg"), None, "freq", None),
        P(),
        P(("parts", "seg"), None),
        P(("parts", "seg")),
        P(),
    )
    out_specs = P(("parts", "seg"), "freq")
    return jax.shard_map(body, mesh=mesh, in_specs=in_specs, out_specs=out_specs, check_vma=False)
```

```python
import math

import functools

import jax
import jax.numpy as jnp
import numpy as np
from jax import lax
from jax.experimental import pallas as pl
from jax.experimental.pallas import tpu as pltpu
from jax.sharding import PartitionSpec as P

BLOCK = 128
KERNELS = 8
REACH = 4
ROUTE_CAP = 4


def extended(cells, sides, width):
    for axis, dim in sides:
        count = lax.axis_size(axis)
        head = lax.slice_in_dim(cells, 0, width, axis=dim)
        tail = lax.slice_in_dim(cells, cells.shape[dim] - width, cells.shape[dim], axis=dim)
        cells = jnp.concatenate(
            [
                lax.ppermute(tail, axis, [(i, (i + 1) % count) for i in range(count)]),
                cells,
                lax.ppermute(head, axis, [((i + 1) % count, i) for i in range(count)]),
            ],
            axis=dim,
        )
    return cells


def passed_along(block, axis, distance):
    devices = range(lax.axis_size(axis))
    route = [((i - distance) % len(devices), i) for i in devices]
    return lax.ppermute(block, axis, route)


def dft_table(size):
    rows = lax.broadcasted_iota(jnp.int32, (size, size), 0)
    cols = lax.broadcasted_iota(jnp.int32, (size, size), 1)
    angle = (rows * cols % size).astype(jnp.float32) * (2.0 * math.pi / size)
    return (jnp.cos(angle), jnp.sin(angle))


def toeplitz(kernels):
    width = kernels.shape[-1]
    tail = jnp.zeros(kernels.shape[:-1] + (width + 1,), kernels.dtype)
    padded = jnp.concatenate([kernels, tail], -1)
    tiled = jnp.tile(padded, (1, 1, width))[..., : 2 * width * width]
    return tiled.reshape(kernels.shape[:-1] + (width, 2 * width))


def take_blocks(joined, start):
    return lax.dynamic_slice_in_dim(joined, start, joined.shape[0] // 2, 0)


def slide(joined, starts):
    return jax.vmap(jax.vmap(take_blocks))(joined, starts)


def general(samples, kernels, offsets, weight_index, level_weights):
    segs, comps, rows_one, cols_two = samples.shape
    ranks = lax.axis_size("freq")
    here = lax.axis_index("freq")
    size_one = rows_one * ranks
    length = size_one * cols_two
    highest = lax.Precision.HIGHEST
    cos_two, sin_two = dft_table(cols_two)
    stacked = samples.reshape(segs * comps * rows_one, cols_two)
    with_cos = jnp.dot(stacked, cos_two, precision=highest).reshape(samples.shape)
    with_sin = jnp.dot(stacked, sin_two, precision=highest).reshape(samples.shape)
    first_real = with_cos[:, 0] + with_sin[:, 1]
    first_imag = with_cos[:, 1] - with_sin[:, 0]
    row_global = here * rows_one + lax.broadcasted_iota(jnp.int32, (rows_one, cols_two), 0)
    col_global = lax.broadcasted_iota(jnp.int32, (rows_one, cols_two), 1)
    twist = (row_global * col_global % length).astype(jnp.float32) * (2.0 * math.pi / length)
    twist_cos = jnp.cos(twist)
    twist_sin = jnp.sin(twist)
    turned = jnp.stack(
        [
            first_real * twist_cos + first_imag * twist_sin,
            first_imag * twist_cos - first_real * twist_sin,
        ],
        1,
    )
    columns = lax.all_to_all(
        turned.astype(jnp.bfloat16), "freq", split_axis=3, concat_axis=3, tiled=True
    ).astype(turned.dtype)
    width_two = cols_two // ranks
    ordered = columns.reshape(segs, comps, rows_one, ranks, width_two)
    cos_one, sin_one = dft_table(size_one)
    cos_one = cos_one.reshape(ranks, rows_one, size_one)
    sin_one = sin_one.reshape(ranks, rows_one, size_one)
    second_cos = jnp.einsum("scirl,rik->sclk", ordered, cos_one, precision=highest)
    second_sin = jnp.einsum("scirl,rik->sclk", ordered, sin_one, precision=highest)
    second = jnp.stack(
        [second_cos[:, 0] + second_sin[:, 1], second_cos[:, 1] - second_sin[:, 0]], 1
    )
    arrived = lax.all_to_all(
        second.astype(jnp.bfloat16), "freq", split_axis=3, concat_axis=3, tiled=True
    ).astype(second.dtype)
    width_one = size_one // ranks
    spectrum = arrived.reshape(segs, comps, width_two, ranks, width_one)
    spectrum = jnp.transpose(spectrum, (0, 1, 4, 3, 2)).reshape(segs, comps, width_one * cols_two)
    spectrum = (spectrum * (1.0 / math.sqrt(length))).astype(jnp.bfloat16)
    half = BLOCK // 2
    edged = extended(spectrum, (("freq", 2),), half)
    bins_here = spectrum.shape[2]
    count = bins_here // BLOCK
    lower = edged[..., :bins_here].reshape(segs, comps, count, BLOCK)
    upper = edged[..., BLOCK:].reshape(segs, comps, count, BLOCK)
    window = jnp.concatenate([lower, upper], -1)
    bands = toeplitz(kernels)
    real_band = bands[0]
    imag_band = bands[1]
    table = jnp.stack(
        [jnp.stack([real_band, imag_band], 0), jnp.stack([-imag_band, real_band], 0)], 0
    )
    filtered = jnp.einsum("scbm,cokim->skboi", window, table, preferred_element_type=jnp.float32)
    power = (filtered[:, :, :, 0] ** 2 + filtered[:, :, :, 1] ** 2).astype(jnp.bfloat16)
    quotient = jnp.floor_divide(offsets, count)
    remainder = offsets - quotient * count
    following = passed_along(power, "freq", -1)
    inner = slide(jnp.concatenate([power, following], 2), remainder)
    plane_count = segs * KERNELS
    flat = inner.reshape(plane_count, count * BLOCK)
    plane_quot = quotient.reshape(plane_count)
    distances = lax.broadcasted_iota(jnp.int32, (2 * REACH + 1, plane_count), 0) - REACH
    member = (plane_quot[None, :] == distances).astype(jnp.int32)
    place = jnp.cumsum(member, 1) - 1
    slot_ids = lax.broadcasted_iota(jnp.int32, (2 * REACH + 1, ROUTE_CAP, plane_count), 1)
    select = ((member[:, None, :] == 1) & (place[:, None, :] == slot_ids)).astype(jnp.bfloat16)
    packed = jnp.einsum("dcp,pl->dcl", select, flat, preferred_element_type=jnp.float32).astype(
        jnp.bfloat16
    )
    received = []
    for step_index in range(2 * REACH + 1):
        received.append(passed_along(packed[step_index], "freq", -(step_index - REACH)))
    gathered = jnp.stack(received, 0)
    placed = jnp.einsum("dcp,dcl->pl", select, gathered, preferred_element_type=jnp.float32)
    shifted = placed.astype(jnp.bfloat16).reshape(segs, KERNELS, count, BLOCK)
    levels = lax.broadcasted_iota(jnp.int32, (segs, level_weights.shape[0]), 1)
    weights = jnp.sum(jnp.where(weight_index[:, None] == levels, level_weights[None, :], 0.0), 1)
    scale = 1.0 / (segs * lax.axis_size("seg"))
    partial_sum = jnp.sum((weights * scale)[:, None, None, None] * shifted.astype(jnp.float32), 0)
    owned = lax.psum_scatter(
        partial_sum.astype(jnp.bfloat16), "seg", scatter_dimension=0, tiled=True
    ).astype(jnp.float32)
    return owned.reshape(owned.shape[0], count * BLOCK)


VMEM = pl.BlockSpec(memory_space=pltpu.VMEM)
SMEM = pl.BlockSpec(memory_space=pltpu.SMEM)
PAD = 16
BF16 = jnp.bfloat16
F32 = jnp.float32


def unit(turns, scale=1.0):
    angle = 2.0 * np.pi * turns
    return (np.cos(angle) * scale).astype(np.float32), (np.sin(angle) * scale).astype(np.float32)


def wave_bases(size, first):
    step = math.isqrt(size)
    while size % step:
        step -= 1
    cols = np.arange(size) + first
    low = np.arange(step)[:, None] * cols[None, :] % size / size
    high = np.arange(size // step)[:, None] * step * cols[None, :] % size / size
    return unit(low) + unit(high)


def fill_waves(low_cos, low_sin, high_cos, high_sin, cos_ref, sin_ref):
    step = low_cos.shape[0]

    @pl.loop(0, high_cos.shape[0])
    def _(i):
        hc = high_cos[pl.ds(i, 1), :]
        hs = high_sin[pl.ds(i, 1), :]
        lc = low_cos[...]
        ls = low_sin[...]
        rows = pl.ds(pl.multiple_of(i * step, step), step)
        cos_ref[rows, :] = (hc * lc - hs * ls).astype(BF16)
        sin_ref[rows, :] = (hs * lc + hc * ls).astype(BF16)


def fill_bands(taps_ref, band_ref):
    wide = 2 * BLOCK
    for t in range(taps_ref.shape[1]):
        both = []
        for c in range(2):
            row = taps_ref[c, t : t + 1, :].astype(F32)
            row = jnp.concatenate([row, jnp.zeros_like(row)], 1)
            row = jnp.broadcast_to(row, (BLOCK, wide))
            both.append(pltpu.roll(row, 0, 1, stride=1, stride_axis=0).T)
        re, im = both
        band_ref[t, :wide, :BLOCK] = re.astype(BF16)
        band_ref[t, :wide, BLOCK:] = im.astype(BF16)
        band_ref[t, wide:, :BLOCK] = (-im).astype(BF16)
        band_ref[t, wide:, BLOCK:] = re.astype(BF16)


def remote(src, dst, sems, at, axis, device):
    return pltpu.make_async_remote_copy(
        src_ref=src,
        dst_ref=dst,
        send_sem=sems[0].at[at],
        recv_sem=sems[1].at[at],
        device_id={axis: device},
        device_id_type=pl.DeviceIdType.MESH,
    )


def first_step(s, x_ref, cos_ref, sin_ref, xb_ref, near_cos, near_sin, far_ref, j):
    rows = x_ref.shape[2]
    lanes = pl.ds(pl.multiple_of(j * BLOCK, BLOCK), BLOCK)
    rhs = jnp.concatenate([cos_ref[:, lanes], sin_ref[:, lanes]], 1)
    got = jnp.dot(xb_ref[s], rhs, preferred_element_type=F32)
    a = far_ref[0:1, lanes]
    b = far_ref[8:9, lanes]
    wc = a * near_cos[:, lanes] - b * near_sin[:, lanes]
    ws = b * near_cos[:, lanes] + a * near_sin[:, lanes]
    re = got[:rows, :BLOCK] + got[rows:, BLOCK:]
    im = got[rows:, :BLOCK] - got[:rows, BLOCK:]
    return jnp.concatenate([re * wc + im * ws, im * wc - re * ws], 1).astype(BF16)


def second_step(s, cos_ref, sin_ref, rhs_ref, w_ref, me, ranks):
    rows = cos_ref.shape[0] // ranks

    @pl.loop(0, ranks)
    def _(i):
        here = pl.ds(pl.multiple_of(i * rows, rows), rows)
        yc = jnp.dot(cos_ref[here, :], rhs_ref[s], preferred_element_type=F32)
        ys = jnp.dot(sin_ref[here, :], rhs_ref[s], preferred_element_type=F32)
        w_ref[0, me, here, :] = (yc[:, :BLOCK] + ys[:, BLOCK:]).astype(BF16)
        w_ref[1, me, here, :] = (yc[:, BLOCK:] - ys[:, :BLOCK]).astype(BF16)


def pad_edges(w_ref, total, ranks):
    tall = w_ref.shape[2] - total
    for c in range(2):
        x = w_ref[c, 0, :total, :].astype(F32)
        w_ref[c, ranks, :total, :] = jnp.concatenate([x[1:], x[:1]], 0).astype(BF16)
        for j in range(ranks + 1):
            w_ref[c, j, total:, :] = w_ref[c, j, :tall, :]


def filter_one(w_ref, band_ref, p_ref, off_ref, s, t, rows, ranks):
    total = rows * ranks
    here = lax.axis_index("freq")
    blocks = total * ranks
    base = lax.rem(here * total + off_ref[s, t] + blocks, blocks)
    gk = base // ranks
    gj = base - gk * ranks
    tall = rows + PAD
    parts = []
    shifts = []
    for jj in range(ranks):
        carry = (gj + jj) // ranks
        j = gj + jj - carry * ranks
        row = lax.rem(gk + carry, total)
        low = row // PAD * PAD
        shifts.append(row - low)
        take = pl.ds(pl.multiple_of(low, PAD), tall)
        pieces = [w_ref[0, j, take, :], w_ref[0, j + 1, take, :], w_ref[1, j, take, :], w_ref[1, j + 1, take, :]]
        parts.append(jnp.concatenate(pieces, 1))
    got = jnp.dot(jnp.concatenate(parts, 0), band_ref[t], preferred_element_type=F32)
    re = got[:, :BLOCK]
    im = got[:, BLOCK:]
    p_ref[...] = re * re + im * im
    return [p_ref[pl.ds(jj * tall + shifts[jj], rows), :] for jj in range(ranks)]


def gather_kernel(
    marks,
    x_hbm, table_hbm, taps_hbm,
    w_first, w_second, band_ref,
    x_ref, table_ref, taps_ref, cos_ref, sin_ref, xb_ref, far_ref, turned, rhs_ref,
    in_sem,
    ex_send, ex_recv, up_send, up_recv, down_send, down_recv,
):
    segs, comps, rows, cols = x_ref.shape
    ranks = lax.axis_size("freq")
    total = rows * ranks
    me = lax.axis_index("freq")
    w_refs = (w_first, w_second)
    exchange = (ex_send, ex_recv)

    fetch_table = pltpu.make_async_copy(table_hbm, table_ref, in_sem.at[0])
    fetch_table.start()
    fetch_x = pltpu.make_async_copy(x_hbm, x_ref, in_sem.at[1])
    fetch_x.start()
    fetch_taps = pltpu.make_async_copy(taps_hbm, taps_ref, in_sem.at[2])
    fetch_taps.start()
    tables = [table_ref.at[marks[i] : marks[i + 1], :] for i in range(len(marks) - 1)]
    b_lc, b_ls, b_hc, b_hs, e_lc, e_ls, e_hc, e_hs, near_cos, near_sin, far_cos, far_sin = tables
    barrier = pltpu.get_barrier_semaphore()
    for d in range(1, ranks):
        peer = (me + d) % ranks
        pl.semaphore_signal(barrier, inc=1, device_id={"freq": peer}, device_id_type=pl.DeviceIdType.MESH)
    pl.semaphore_wait(barrier, ranks - 1)

    fetch_table.wait()
    fill_waves(b_lc, b_ls, b_hc, b_hs, cos_ref, sin_ref)
    fetch_x.wait()
    far_ref[0:1, :] = far_cos[pl.ds(me, 1), :]
    far_ref[8:9, :] = far_sin[pl.ds(me, 1), :]
    for s in range(segs):
        for c in range(comps):
            xb_ref[s, c * rows : (c + 1) * rows, :] = x_ref[s, c].astype(BF16)

    def sent(s, d):
        here = pl.ds(pl.multiple_of(me * rows, rows), rows)
        return remote(turned.at[s, d], rhs_ref.at[s, here, :], exchange, (s, d), "freq", (me + d) % ranks)

    def own_rows():
        return pl.ds(pl.multiple_of(me * rows, rows), rows)

    for s in range(segs):
        step = functools.partial(first_step, s, x_ref, cos_ref, sin_ref, xb_ref, near_cos, near_sin, far_ref)

        @pl.loop(1, ranks)
        def _(d):
            turned[s, d] = step((me + d) % ranks)
            sent(s, d).start()

        rhs_ref[s, own_rows(), :] = step(me)

    fill_waves(e_lc, e_ls, e_hc, e_hs, cos_ref, sin_ref)
    fetch_taps.wait()
    fill_bands(taps_ref, band_ref)

    odd = me % 2
    place = (1 - odd) * (me // 2) + odd * (ranks - 1 - me // 2)

    def at_place(p):
        p = (p + ranks) % ranks
        far = p // (ranks // 2)
        return (1 - far) * (2 * p) + far * (2 * (ranks - 1 - p) + 1)

    mid = total // 2

    def hop(s, c, k, way):
        owner = at_place(place - k) if way == 0 else at_place(place + k)
        target = at_place(place + 1) if way == 0 else at_place(place - 1)
        block = w_refs[s].at[c, owner, pl.ds(way * mid, mid), :]
        sems = ((up_send, up_recv), (down_send, down_recv))[way]
        return remote(block, block, sems, (s, c, k), "freq", target)

    def landed(s, c, k, way):
        owner = at_place(place - k - 1) if way == 0 else at_place(place + k + 1)
        target = at_place(place + 1) if way == 0 else at_place(place - 1)
        block = w_refs[s].at[c, owner, pl.ds(way * mid, mid), :]
        sems = ((up_send, up_recv), (down_send, down_recv))[way]
        return remote(block, block, sems, (s, c, k), "freq", target)

    def advance(s, k):
        for c in range(comps):
            for way in range(2):
                landed(s, c, k - 1, way).wait_recv()
                if k < ranks - 1:
                    hop(s, c, k, way).start()

    for s in range(segs):
        for d in range(1, ranks):
            here = pl.ds(pl.multiple_of((me + ranks - d) % ranks * rows, rows), rows)
            remote(turned.at[s, d], rhs_ref.at[s, here, :], exchange, (s, d), "freq", (me + d) % ranks).wait_recv()
        second_step(s, cos_ref, sin_ref, rhs_ref, w_refs[s], me, ranks)
        for c in range(comps):
            for way in range(2):
                hop(s, c, 0, way).start()
        if s == 0:
            advance(0, 1)

    for k in range(1, ranks):
        if k + 1 < ranks:
            advance(0, k + 1)
        else:
            pad_edges(w_refs[0], total, ranks)
        advance(1, k)
    pad_edges(w_refs[1], total, ranks)

    for s in range(segs):
        for d in range(1, ranks):
            sent(s, d).wait_send()
        for c in range(comps):
            for k in range(ranks - 1):
                for way in range(2):
                    hop(s, c, k, way).wait_send()


def filter_kernel(own, off_ref, wi_ref, lw_ref, w_first, w_second, band_ref, out_ref, p_ref):
    half, rows, cols = out_ref.shape
    ranks = cols // BLOCK
    w_refs = (w_first, w_second)
    scale = 1.0 / (2 * len(w_refs))
    core = lax.axis_index("seg")
    weights = [lw_ref[wi_ref[s]] * scale for s in range(len(w_refs))]
    first = (core if own else 1 - core) * half

    @pl.loop(0, half)
    def _(i):
        sums = None
        for s, w_ref in enumerate(w_refs):
            got = filter_one(w_ref, band_ref, p_ref.at[s], off_ref, s, first + i, rows, ranks)
            got = [weights[s] * x for x in got]
            sums = got if sums is None else [x + y for x, y in zip(sums, got)]
        for jj in range(ranks):
            out_ref[i, :, jj * BLOCK : (jj + 1) * BLOCK] = sums[jj].astype(out_ref.dtype)


def body(samples, kernels, offsets, weight_index, level_weights):
    segs, comps, rows, cols = samples.shape
    ranks = lax.axis_size("freq")
    size_one = rows * ranks
    if cols != ranks * BLOCK or rows != BLOCK or size_one != cols or segs != 2 or lax.axis_size("seg") != 2:
        return general(samples, kernels, offsets, weight_index, level_weights)
    length = size_one * cols
    bins = np.arange(cols) - BLOCK // 2
    near = unit(np.arange(rows)[:, None] * bins[None, :] % length / length, 1.0 / math.sqrt(length))
    far = unit(np.arange(ranks)[:, None] * rows * bins[None, :] % length / length)
    half = kernels.shape[1] // 2
    tall = rows + PAD
    copies = pltpu.SemaphoreType.DMA
    gathered = jax.ShapeDtypeStruct((comps, ranks + 1, size_one + tall, BLOCK), BF16)
    bands = jax.ShapeDtypeStruct((kernels.shape[1], 4 * BLOCK, 2 * BLOCK), BF16)
    tables = (*wave_bases(cols, -(BLOCK // 2)), *wave_bases(size_one, 0), *near, *far)
    marks = np.cumsum([0] + [len(x) for x in tables]).tolist()
    first, second, bands = pl.pallas_call(
        functools.partial(gather_kernel, marks),
        out_shape=(gathered, gathered, bands),
        in_specs=[pl.BlockSpec(memory_space=pltpu.HBM)] * 3,
        out_specs=(VMEM, VMEM, VMEM),
        scratch_shapes=[pltpu.VMEM(samples.shape, F32), pltpu.VMEM((marks[-1], cols), F32)]
        + [pltpu.VMEM(kernels.shape, kernels.dtype)]
        + [pltpu.VMEM((cols, cols), BF16)] * 2
        + [
            pltpu.VMEM((segs, comps * rows, cols), BF16),
            pltpu.VMEM((16, cols), F32),
            pltpu.VMEM((segs, ranks, rows, 2 * BLOCK), BF16),
            pltpu.VMEM((segs, size_one, 2 * BLOCK), BF16),
        ]
        + [copies((3,))]
        + [copies((segs, ranks))] * 2
        + [copies((segs, comps, ranks - 1))] * 4,
        compiler_params=pltpu.CompilerParams(vmem_limit_bytes=36 << 20, collective_id=0, has_side_effects=True),
    )(
        pltpu.with_memory_space_constraint(samples, pltpu.HBM),
        pltpu.with_memory_space_constraint(jnp.asarray(np.concatenate(tables)), pltpu.HBM),
        pltpu.with_memory_space_constraint(kernels, pltpu.HBM),
    )

    def filtered(own, kind):
        flops = 2 * 8 * half * segs * ranks * tall * BLOCK * BLOCK
        return pl.pallas_call(
            functools.partial(filter_kernel, own),
            out_shape=jax.ShapeDtypeStruct((half, rows, cols), kind),
            in_specs=[SMEM] * 3 + [VMEM] * 3,
            out_specs=VMEM,
            scratch_shapes=[pltpu.VMEM((segs, ranks * tall, BLOCK), F32)],
            compiler_params=pltpu.CompilerParams(vmem_limit_bytes=24 << 20),
            cost_estimate=pl.CostEstimate(flops=flops, bytes_accessed=8 << 20, transcendentals=0),
        )(offsets, weight_index, level_weights, first, second, bands)

    swapped = lax.ppermute(filtered(False, BF16), "seg", [(0, 1), (1, 0)])
    return (filtered(True, F32) + swapped.astype(F32)).reshape(half, rows * cols)


def solution(mesh):
    in_specs = (
        P(("parts", "seg"), None, "freq", None),
        P(),
        P(("parts", "seg"), None),
        P(("parts", "seg")),
        P(),
    )
    out_specs = P(("parts", "seg"), "freq")
    return jax.shard_map(body, mesh=mesh, in_specs=in_specs, out_specs=out_specs, check_vma=False)
```

```python
import math

import functools

import jax
import jax.numpy as jnp
import numpy as np
from jax import lax
from jax.experimental import pallas as pl
from jax.experimental.pallas import tpu as pltpu
from jax.sharding import PartitionSpec as P

BLOCK = 128
KERNELS = 8
REACH = 4
ROUTE_CAP = 4


def extended(cells, sides, width):
    for axis, dim in sides:
        count = lax.axis_size(axis)
        head = lax.slice_in_dim(cells, 0, width, axis=dim)
        tail = lax.slice_in_dim(cells, cells.shape[dim] - width, cells.shape[dim], axis=dim)
        cells = jnp.concatenate(
            [
                lax.ppermute(tail, axis, [(i, (i + 1) % count) for i in range(count)]),
                cells,
                lax.ppermute(head, axis, [((i + 1) % count, i) for i in range(count)]),
            ],
            axis=dim,
        )
    return cells


def passed_along(block, axis, distance):
    devices = range(lax.axis_size(axis))
    route = [((i - distance) % len(devices), i) for i in devices]
    return lax.ppermute(block, axis, route)


def dft_table(size):
    rows = lax.broadcasted_iota(jnp.int32, (size, size), 0)
    cols = lax.broadcasted_iota(jnp.int32, (size, size), 1)
    angle = (rows * cols % size).astype(jnp.float32) * (2.0 * math.pi / size)
    return (jnp.cos(angle), jnp.sin(angle))


def toeplitz(kernels):
    width = kernels.shape[-1]
    tail = jnp.zeros(kernels.shape[:-1] + (width + 1,), kernels.dtype)
    padded = jnp.concatenate([kernels, tail], -1)
    tiled = jnp.tile(padded, (1, 1, width))[..., : 2 * width * width]
    return tiled.reshape(kernels.shape[:-1] + (width, 2 * width))


def take_blocks(joined, start):
    return lax.dynamic_slice_in_dim(joined, start, joined.shape[0] // 2, 0)


def slide(joined, starts):
    return jax.vmap(jax.vmap(take_blocks))(joined, starts)


def general(samples, kernels, offsets, weight_index, level_weights):
    segs, comps, rows_one, cols_two = samples.shape
    ranks = lax.axis_size("freq")
    here = lax.axis_index("freq")
    size_one = rows_one * ranks
    length = size_one * cols_two
    highest = lax.Precision.HIGHEST
    cos_two, sin_two = dft_table(cols_two)
    stacked = samples.reshape(segs * comps * rows_one, cols_two)
    with_cos = jnp.dot(stacked, cos_two, precision=highest).reshape(samples.shape)
    with_sin = jnp.dot(stacked, sin_two, precision=highest).reshape(samples.shape)
    first_real = with_cos[:, 0] + with_sin[:, 1]
    first_imag = with_cos[:, 1] - with_sin[:, 0]
    row_global = here * rows_one + lax.broadcasted_iota(jnp.int32, (rows_one, cols_two), 0)
    col_global = lax.broadcasted_iota(jnp.int32, (rows_one, cols_two), 1)
    twist = (row_global * col_global % length).astype(jnp.float32) * (2.0 * math.pi / length)
    twist_cos = jnp.cos(twist)
    twist_sin = jnp.sin(twist)
    turned = jnp.stack(
        [
            first_real * twist_cos + first_imag * twist_sin,
            first_imag * twist_cos - first_real * twist_sin,
        ],
        1,
    )
    columns = lax.all_to_all(
        turned.astype(jnp.bfloat16), "freq", split_axis=3, concat_axis=3, tiled=True
    ).astype(turned.dtype)
    width_two = cols_two // ranks
    ordered = columns.reshape(segs, comps, rows_one, ranks, width_two)
    cos_one, sin_one = dft_table(size_one)
    cos_one = cos_one.reshape(ranks, rows_one, size_one)
    sin_one = sin_one.reshape(ranks, rows_one, size_one)
    second_cos = jnp.einsum("scirl,rik->sclk", ordered, cos_one, precision=highest)
    second_sin = jnp.einsum("scirl,rik->sclk", ordered, sin_one, precision=highest)
    second = jnp.stack(
        [second_cos[:, 0] + second_sin[:, 1], second_cos[:, 1] - second_sin[:, 0]], 1
    )
    arrived = lax.all_to_all(
        second.astype(jnp.bfloat16), "freq", split_axis=3, concat_axis=3, tiled=True
    ).astype(second.dtype)
    width_one = size_one // ranks
    spectrum = arrived.reshape(segs, comps, width_two, ranks, width_one)
    spectrum = jnp.transpose(spectrum, (0, 1, 4, 3, 2)).reshape(segs, comps, width_one * cols_two)
    spectrum = (spectrum * (1.0 / math.sqrt(length))).astype(jnp.bfloat16)
    half = BLOCK // 2
    edged = extended(spectrum, (("freq", 2),), half)
    bins_here = spectrum.shape[2]
    count = bins_here // BLOCK
    lower = edged[..., :bins_here].reshape(segs, comps, count, BLOCK)
    upper = edged[..., BLOCK:].reshape(segs, comps, count, BLOCK)
    window = jnp.concatenate([lower, upper], -1)
    bands = toeplitz(kernels)
    real_band = bands[0]
    imag_band = bands[1]
    table = jnp.stack(
        [jnp.stack([real_band, imag_band], 0), jnp.stack([-imag_band, real_band], 0)], 0
    )
    filtered = jnp.einsum("scbm,cokim->skboi", window, table, preferred_element_type=jnp.float32)
    power = (filtered[:, :, :, 0] ** 2 + filtered[:, :, :, 1] ** 2).astype(jnp.bfloat16)
    quotient = jnp.floor_divide(offsets, count)
    remainder = offsets - quotient * count
    following = passed_along(power, "freq", -1)
    inner = slide(jnp.concatenate([power, following], 2), remainder)
    plane_count = segs * KERNELS
    flat = inner.reshape(plane_count, count * BLOCK)
    plane_quot = quotient.reshape(plane_count)
    distances = lax.broadcasted_iota(jnp.int32, (2 * REACH + 1, plane_count), 0) - REACH
    member = (plane_quot[None, :] == distances).astype(jnp.int32)
    place = jnp.cumsum(member, 1) - 1
    slot_ids = lax.broadcasted_iota(jnp.int32, (2 * REACH + 1, ROUTE_CAP, plane_count), 1)
    select = ((member[:, None, :] == 1) & (place[:, None, :] == slot_ids)).astype(jnp.bfloat16)
    packed = jnp.einsum("dcp,pl->dcl", select, flat, preferred_element_type=jnp.float32).astype(
        jnp.bfloat16
    )
    received = []
    for step_index in range(2 * REACH + 1):
        received.append(passed_along(packed[step_index], "freq", -(step_index - REACH)))
    gathered = jnp.stack(received, 0)
    placed = jnp.einsum("dcp,dcl->pl", select, gathered, preferred_element_type=jnp.float32)
    shifted = placed.astype(jnp.bfloat16).reshape(segs, KERNELS, count, BLOCK)
    levels = lax.broadcasted_iota(jnp.int32, (segs, level_weights.shape[0]), 1)
    weights = jnp.sum(jnp.where(weight_index[:, None] == levels, level_weights[None, :], 0.0), 1)
    scale = 1.0 / (segs * lax.axis_size("seg"))
    partial_sum = jnp.sum((weights * scale)[:, None, None, None] * shifted.astype(jnp.float32), 0)
    owned = lax.psum_scatter(
        partial_sum.astype(jnp.bfloat16), "seg", scatter_dimension=0, tiled=True
    ).astype(jnp.float32)
    return owned.reshape(owned.shape[0], count * BLOCK)


VMEM = pl.BlockSpec(memory_space=pltpu.VMEM)
SMEM = pl.BlockSpec(memory_space=pltpu.SMEM)
PAD = 16
BF16 = jnp.bfloat16
F32 = jnp.float32


def unit(turns, scale=1.0):
    angle = 2.0 * np.pi * turns
    return (np.cos(angle) * scale).astype(np.float32), (np.sin(angle) * scale).astype(np.float32)


def wave_bases(size, first):
    step = math.isqrt(size)
    while size % step:
        step -= 1
    cols = np.arange(size) + first
    low = np.arange(step)[:, None] * cols[None, :] % size / size
    high = np.arange(size // step)[:, None] * step * cols[None, :] % size / size
    return unit(low) + unit(high)


def fill_waves(low_cos, low_sin, high_cos, high_sin, cos_ref, sin_ref):
    step = low_cos.shape[0]

    @pl.loop(0, high_cos.shape[0])
    def _(i):
        hc = high_cos[pl.ds(i, 1), :]
        hs = high_sin[pl.ds(i, 1), :]
        lc = low_cos[...]
        ls = low_sin[...]
        rows = pl.ds(pl.multiple_of(i * step, step), step)
        cos_ref[rows, :] = (hc * lc - hs * ls).astype(BF16)
        sin_ref[rows, :] = (hs * lc + hc * ls).astype(BF16)


def fill_bands(taps_ref, band_ref):
    wide = 2 * BLOCK
    for t in range(taps_ref.shape[1]):
        both = []
        for c in range(2):
            row = taps_ref[c, t : t + 1, :].astype(F32)
            row = jnp.concatenate([row, jnp.zeros_like(row)], 1)
            row = jnp.broadcast_to(row, (BLOCK, wide))
            both.append(pltpu.roll(row, 0, 1, stride=1, stride_axis=0).T)
        re, im = both
        band_ref[t, :wide, :BLOCK] = re.astype(BF16)
        band_ref[t, :wide, BLOCK:] = im.astype(BF16)
        band_ref[t, wide:, :BLOCK] = (-im).astype(BF16)
        band_ref[t, wide:, BLOCK:] = re.astype(BF16)


def fill_columns(low_cos, low_sin, high_cos, high_sin, cos_ref, sin_ref, j):
    step = low_cos.shape[0]
    lanes = pl.ds(pl.multiple_of(j * BLOCK, BLOCK), BLOCK)
    lc = low_cos[:, lanes]
    ls = low_sin[:, lanes]
    for i in range(high_cos.shape[0]):
        hc = high_cos[i : i + 1, lanes]
        hs = high_sin[i : i + 1, lanes]
        rows = slice(i * step, (i + 1) * step)
        cos_ref[rows, lanes] = (hc * lc - hs * ls).astype(BF16)
        sin_ref[rows, lanes] = (hs * lc + hc * ls).astype(BF16)


def remote(src, dst, sems, at, axis, device):
    return pltpu.make_async_remote_copy(
        src_ref=src,
        dst_ref=dst,
        send_sem=sems[0].at[at],
        recv_sem=sems[1].at[at],
        device_id={axis: device},
        device_id_type=pl.DeviceIdType.MESH,
    )


def first_step(s, x_ref, cos_ref, sin_ref, xb_ref, near_cos, near_sin, far_ref, j):
    rows = x_ref.shape[2]
    lanes = pl.ds(pl.multiple_of(j * BLOCK, BLOCK), BLOCK)
    rhs = jnp.concatenate([cos_ref[:, lanes], sin_ref[:, lanes]], 1)
    got = jnp.dot(xb_ref[s], rhs, preferred_element_type=F32)
    a = far_ref[0:1, lanes]
    b = far_ref[8:9, lanes]
    wc = a * near_cos[:, lanes] - b * near_sin[:, lanes]
    ws = b * near_cos[:, lanes] + a * near_sin[:, lanes]
    re = got[:rows, :BLOCK] + got[rows:, BLOCK:]
    im = got[rows:, :BLOCK] - got[:rows, BLOCK:]
    return jnp.concatenate([re * wc + im * ws, im * wc - re * ws], 1).astype(BF16)


def second_step(s, cos_ref, sin_ref, rhs_ref, w_ref, me, ranks):
    rows = cos_ref.shape[0] // ranks

    @pl.loop(0, ranks)
    def _(i):
        here = pl.ds(pl.multiple_of(i * rows, rows), rows)
        yc = jnp.dot(cos_ref[here, :], rhs_ref[s], preferred_element_type=F32)
        ys = jnp.dot(sin_ref[here, :], rhs_ref[s], preferred_element_type=F32)
        w_ref[0, me, here, :] = (yc[:, :BLOCK] + ys[:, BLOCK:]).astype(BF16)
        w_ref[1, me, here, :] = (yc[:, BLOCK:] - ys[:, :BLOCK]).astype(BF16)


def pad_edges(w_ref, total, ranks):
    tall = w_ref.shape[2] - total
    for c in range(2):
        x = w_ref[c, 0, :total, :].astype(F32)
        w_ref[c, ranks, :total, :] = jnp.concatenate([x[1:], x[:1]], 0).astype(BF16)
        for j in range(ranks + 1):
            w_ref[c, j, total:, :] = w_ref[c, j, :tall, :]


def filter_one(w_ref, band_ref, p_ref, off_ref, s, t, rows, ranks):
    total = rows * ranks
    here = lax.axis_index("freq")
    blocks = total * ranks
    base = lax.rem(here * total + off_ref[s, t] + blocks, blocks)
    gk = base // ranks
    gj = base - gk * ranks
    tall = rows + PAD
    parts = []
    shifts = []
    for jj in range(ranks):
        carry = (gj + jj) // ranks
        j = gj + jj - carry * ranks
        row = lax.rem(gk + carry, total)
        low = row // PAD * PAD
        shifts.append(row - low)
        take = pl.ds(pl.multiple_of(low, PAD), tall)
        pieces = [w_ref[0, j, take, :], w_ref[0, j + 1, take, :], w_ref[1, j, take, :], w_ref[1, j + 1, take, :]]
        parts.append(jnp.concatenate(pieces, 1))
    got = jnp.dot(jnp.concatenate(parts, 0), band_ref[t], preferred_element_type=F32)
    re = got[:, :BLOCK]
    im = got[:, BLOCK:]
    p_ref[...] = re * re + im * im
    return [p_ref[pl.ds(jj * tall + shifts[jj], rows), :] for jj in range(ranks)]


def gather_kernel(
    marks,
    x_hbm, table_hbm, taps_hbm,
    w_first, w_second, band_ref,
    x_ref, table_ref, taps_ref, cos_ref, sin_ref, xb_ref, far_ref, turned, rhs_ref,
    in_sem,
    ex_send, ex_recv, up_send, up_recv, down_send, down_recv,
):
    segs, comps, rows, cols = x_ref.shape
    ranks = lax.axis_size("freq")
    total = rows * ranks
    me = lax.axis_index("freq")
    w_refs = (w_first, w_second)
    exchange = (ex_send, ex_recv)

    fetch_table = pltpu.make_async_copy(table_hbm, table_ref, in_sem.at[0])
    fetch_table.start()
    fetch_x = pltpu.make_async_copy(x_hbm, x_ref, in_sem.at[1])
    fetch_x.start()
    fetch_taps = pltpu.make_async_copy(taps_hbm, taps_ref, in_sem.at[2])
    fetch_taps.start()
    tables = [table_ref.at[marks[i] : marks[i + 1], :] for i in range(len(marks) - 1)]
    b_lc, b_ls, b_hc, b_hs, e_lc, e_ls, e_hc, e_hs, near_cos, near_sin, far_cos, far_sin = tables
    barrier = pltpu.get_barrier_semaphore()
    for d in range(1, ranks):
        peer = (me + d) % ranks
        pl.semaphore_signal(barrier, inc=1, device_id={"freq": peer}, device_id_type=pl.DeviceIdType.MESH)
    pl.semaphore_wait(barrier, ranks - 1)

    fetch_table.wait()
    fetch_x.wait()
    far_ref[0:1, :] = far_cos[pl.ds(me, 1), :]
    far_ref[8:9, :] = far_sin[pl.ds(me, 1), :]
    for s in range(segs):
        for c in range(comps):
            xb_ref[s, c * rows : (c + 1) * rows, :] = x_ref[s, c].astype(BF16)

    def sent(s, d):
        here = pl.ds(pl.multiple_of(me * rows, rows), rows)
        return remote(turned.at[s, d], rhs_ref.at[s, here, :], exchange, (s, d), "freq", (me + d) % ranks)

    def own_rows():
        return pl.ds(pl.multiple_of(me * rows, rows), rows)

    for s in range(segs):
        step = functools.partial(first_step, s, x_ref, cos_ref, sin_ref, xb_ref, near_cos, near_sin, far_ref)

        @pl.loop(1, ranks)
        def _(d):
            if s == 0:
                fill_columns(b_lc, b_ls, b_hc, b_hs, cos_ref, sin_ref, (me + d) % ranks)
            turned[s, d] = step((me + d) % ranks)
            sent(s, d).start()

        if s == 0:
            fill_columns(b_lc, b_ls, b_hc, b_hs, cos_ref, sin_ref, me)
        rhs_ref[s, own_rows(), :] = step(me)

    fill_waves(e_lc, e_ls, e_hc, e_hs, cos_ref, sin_ref)
    fetch_taps.wait()
    fill_bands(taps_ref, band_ref)

    odd = me % 2
    place = (1 - odd) * (me // 2) + odd * (ranks - 1 - me // 2)

    def at_place(p):
        p = (p + ranks) % ranks
        far = p // (ranks // 2)
        return (1 - far) * (2 * p) + far * (2 * (ranks - 1 - p) + 1)

    mid = total // 2

    def hop(s, c, k, way):
        owner = at_place(place - k) if way == 0 else at_place(place + k)
        target = at_place(place + 1) if way == 0 else at_place(place - 1)
        block = w_refs[s].at[c, owner, pl.ds(way * mid, mid), :]
        sems = ((up_send, up_recv), (down_send, down_recv))[way]
        return remote(block, block, sems, (s, c, k), "freq", target)

    def landed(s, c, k, way):
        owner = at_place(place - k - 1) if way == 0 else at_place(place + k + 1)
        target = at_place(place + 1) if way == 0 else at_place(place - 1)
        block = w_refs[s].at[c, owner, pl.ds(way * mid, mid), :]
        sems = ((up_send, up_recv), (down_send, down_recv))[way]
        return remote(block, block, sems, (s, c, k), "freq", target)

    def advance(s, k):
        for c in range(comps):
            for way in range(2):
                landed(s, c, k - 1, way).wait_recv()
                if k < ranks - 1:
                    hop(s, c, k, way).start()

    for s in range(segs):
        for d in range(1, ranks):
            here = pl.ds(pl.multiple_of((me + ranks - d) % ranks * rows, rows), rows)
            remote(turned.at[s, d], rhs_ref.at[s, here, :], exchange, (s, d), "freq", (me + d) % ranks).wait_recv()
        second_step(s, cos_ref, sin_ref, rhs_ref, w_refs[s], me, ranks)
        for c in range(comps):
            for way in range(2):
                hop(s, c, 0, way).start()
        if s == 0:
            advance(0, 1)

    for k in range(1, ranks):
        if k + 1 < ranks:
            advance(0, k + 1)
        else:
            pad_edges(w_refs[0], total, ranks)
        advance(1, k)
    pad_edges(w_refs[1], total, ranks)

    for s in range(segs):
        for d in range(1, ranks):
            sent(s, d).wait_send()
        for c in range(comps):
            for k in range(ranks - 1):
                for way in range(2):
                    hop(s, c, k, way).wait_send()


def filter_kernel(own, off_ref, wi_ref, lw_ref, w_first, w_second, band_ref, out_ref, p_ref):
    half, rows, cols = out_ref.shape
    ranks = cols // BLOCK
    w_refs = (w_first, w_second)
    scale = 1.0 / (2 * len(w_refs))
    core = lax.axis_index("seg")
    weights = [lw_ref[wi_ref[s]] * scale for s in range(len(w_refs))]
    first = (core if own else 1 - core) * half

    @pl.loop(0, half)
    def _(i):
        sums = None
        for s, w_ref in enumerate(w_refs):
            got = filter_one(w_ref, band_ref, p_ref.at[s], off_ref, s, first + i, rows, ranks)
            got = [weights[s] * x for x in got]
            sums = got if sums is None else [x + y for x, y in zip(sums, got)]
        for jj in range(ranks):
            out_ref[i, :, jj * BLOCK : (jj + 1) * BLOCK] = sums[jj].astype(out_ref.dtype)


def body(samples, kernels, offsets, weight_index, level_weights):
    segs, comps, rows, cols = samples.shape
    ranks = lax.axis_size("freq")
    size_one = rows * ranks
    if cols != ranks * BLOCK or rows != BLOCK or size_one != cols or segs != 2 or lax.axis_size("seg") != 2:
        return general(samples, kernels, offsets, weight_index, level_weights)
    length = size_one * cols
    bins = np.arange(cols) - BLOCK // 2
    near = unit(np.arange(rows)[:, None] * bins[None, :] % length / length, 1.0 / math.sqrt(length))
    far = unit(np.arange(ranks)[:, None] * rows * bins[None, :] % length / length)
    half = kernels.shape[1] // 2
    tall = rows + PAD
    copies = pltpu.SemaphoreType.DMA
    gathered = jax.ShapeDtypeStruct((comps, ranks + 1, size_one + tall, BLOCK), BF16)
    bands = jax.ShapeDtypeStruct((kernels.shape[1], 4 * BLOCK, 2 * BLOCK), BF16)
    tables = (*wave_bases(cols, -(BLOCK // 2)), *wave_bases(size_one, 0), *near, *far)
    marks = np.cumsum([0] + [len(x) for x in tables]).tolist()
    first, second, bands = pl.pallas_call(
        functools.partial(gather_kernel, marks),
        out_shape=(gathered, gathered, bands),
        in_specs=[pl.BlockSpec(memory_space=pltpu.HBM)] * 3,
        out_specs=(VMEM, VMEM, VMEM),
        scratch_shapes=[pltpu.VMEM(samples.shape, F32), pltpu.VMEM((marks[-1], cols), F32)]
        + [pltpu.VMEM(kernels.shape, kernels.dtype)]
        + [pltpu.VMEM((cols, cols), BF16)] * 2
        + [
            pltpu.VMEM((segs, comps * rows, cols), BF16),
            pltpu.VMEM((16, cols), F32),
            pltpu.VMEM((segs, ranks, rows, 2 * BLOCK), BF16),
            pltpu.VMEM((segs, size_one, 2 * BLOCK), BF16),
        ]
        + [copies((3,))]
        + [copies((segs, ranks))] * 2
        + [copies((segs, comps, ranks - 1))] * 4,
        compiler_params=pltpu.CompilerParams(vmem_limit_bytes=36 << 20, collective_id=0, has_side_effects=True),
    )(
        pltpu.with_memory_space_constraint(samples, pltpu.HBM),
        pltpu.with_memory_space_constraint(jnp.asarray(np.concatenate(tables)), pltpu.HBM),
        pltpu.with_memory_space_constraint(kernels, pltpu.HBM),
    )

    def filtered(own, kind):
        flops = 2 * 8 * half * segs * ranks * tall * BLOCK * BLOCK
        return pl.pallas_call(
            functools.partial(filter_kernel, own),
            out_shape=jax.ShapeDtypeStruct((half, rows, cols), kind),
            in_specs=[SMEM] * 3 + [VMEM] * 3,
            out_specs=VMEM,
            scratch_shapes=[pltpu.VMEM((segs, ranks * tall, BLOCK), F32)],
            compiler_params=pltpu.CompilerParams(vmem_limit_bytes=24 << 20),
            cost_estimate=pl.CostEstimate(flops=flops, bytes_accessed=8 << 20, transcendentals=0),
        )(offsets, weight_index, level_weights, first, second, bands)

    swapped = lax.ppermute(filtered(False, BF16), "seg", [(0, 1), (1, 0)])
    return (filtered(True, F32) + swapped.astype(F32)).reshape(half, rows * cols)


def solution(mesh):
    in_specs = (
        P(("parts", "seg"), None, "freq", None),
        P(),
        P(("parts", "seg"), None),
        P(("parts", "seg")),
        P(),
    )
    out_specs = P(("parts", "seg"), "freq")
    return jax.shard_map(body, mesh=mesh, in_specs=in_specs, out_specs=out_specs, check_vma=False)
```
